768 devices in a mesh: grp: 48 (over y_lo, z, core), tp: 16 (over x, y_hi).
Axes of the slice: x: 4, y: 8 (y_hi: 4, y_lo: 2; y = y_hi * 2 + y_lo), z: 12, core: 2. Of those that a mesh axis runs over, the one named last changes fastest.
Arguments:
- query_heads: bfloat16 [24576, 4096], P('grp', 'tp'), may hold values from -6 to 6
- key_heads: bfloat16 [24576, 4096], P('grp', 'tp'), may hold values from -6 to 6
- value_heads: bfloat16 [24576, 4096], P('grp', 'tp'), may hold values from -12 to 12
- modality: int32 [48, 768], P('grp'), may hold values from 0 to 1, as said below
- doc_ids: int32 [48, 768], P('grp'), may hold values from 0 to 188, as said below
- out_weight: bfloat16 [2, 4096, 4096], P(None, 'tp'), may hold values from -0.1875 to 0.1875
- out_grad: bfloat16 [24576, 4096], P('grp'), may hold values from -6 to 6
Outputs:
- layer_output: bfloat16 [24576, 4096], P('grp', 'tp')
- grad_query: bfloat16 [24576, 4096], P('grp', 'tp')
- grad_key: bfloat16 [24576, 4096], P('grp', 'tp')
- grad_value: bfloat16 [24576, 4096], P('grp', 'tp')
The draws below stay inside these ranges and needn't reach their ends.
Inputs may be any that keep to these rules, and one draw needn't show every extreme that they name: `modality`: row g and row g + 24 describe the same pack. 0 marks a text position, 1 an image position. Positions 0 to 15 alternate text, image. Every pack holds 256 to 512 text positions; some pack holds exactly 512 text positions and some exactly 512 image positions. `doc_ids`: row g and row g + 24 describe the same pack. The document number is 0 at position 0, never falls and rises by at most one a position; a new document starts only at positions of 16 or more that are multiples of 4.
All inputs are finite; a program needn't handle non-finite values.
Results may differ from the reference program's by a relative error of at most 0.028.
Values may be sent and summed in bfloat16 or wider, within the bound.
No kernel may reach another device: no remote copies, remote signals or barrier semaphores. Data moves between devices by JAX's collectives and lax.ppermute only.
A program may use at most 64 MiB of HBM per device.

```python
import jax
import jax.numpy as jnp
from jax import lax

D = 4096
HEADS = 32
HD = 128
ROWS = 512
PACK = 768
INNER = 4096
ALLROWS = 24576
N_GRP = 48


def pack_layout(seed_key):
    base_key = jax.random.fold_in(seed_key, 7)
    pair_count = N_GRP // 2

    def one_pack(pack_index):
        pack_key = jax.random.fold_in(base_key, pack_index)
        count_key, order_key, start_key = jax.random.split(pack_key, 3)
        text_count = jax.random.randint(count_key, (), PACK - ROWS, ROWS + 1)
        text_count = jnp.where(pack_index == 0, ROWS, jnp.where(pack_index == 1, PACK - ROWS, text_count))
        shuffled = jax.random.permutation(order_key, PACK - 16)
        rest_modal = jnp.where(shuffled < text_count - 8, 0, 1).astype(jnp.int32)
        prefix = jnp.arange(16, dtype=jnp.int32) % 2
        modal_row = jnp.concatenate((prefix, rest_modal))
        spots = jnp.arange(PACK, dtype=jnp.int32)
        eligible = (spots >= 16) & (spots % 4 == 0)
        random_starts = jax.random.randint(start_key, (PACK,), 0, max(PACK // 16, 2)) == 0
        starts = eligible & (random_starts | (pack_index == 0))
        starts = starts | (spots == 0)
        doc_row = (jnp.cumsum(starts.astype(jnp.int32)) - 1).astype(jnp.int32)
        return (modal_row, doc_row)
    modal_rows, doc_rows = jax.vmap(one_pack)(jnp.arange(pair_count, dtype=jnp.int32))
    return (jnp.concatenate((modal_rows, modal_rows)), jnp.concatenate((doc_rows, doc_rows)))


def draw_modality(key, part):
    return pack_layout(key)[0]


def draw_doc_ids(key, part):
    return pack_layout(key)[1]


def draw_query_heads(key, part):
    shape = (N_GRP * ROWS, HEADS * HD)
    own_key = jax.random.fold_in(key, 1)
    result = jnp.clip(jax.random.normal(own_key, shape, jnp.float32), -4.0, 4.0)
    return result.astype(jnp.bfloat16)


def draw_key_heads(key, part):
    shape = (N_GRP * ROWS, HEADS * HD)
    own_key = jax.random.fold_in(key, 2)
    result = jnp.clip(jax.random.normal(own_key, shape, jnp.float32), -4.0, 4.0)
    return result.astype(jnp.bfloat16)


def levels(key, extent, cuts, least, top_value):
    def one(position, parts):
        draws = jax.random.uniform(jax.random.fold_in(jax.random.fold_in(key, 6), position), (parts,), jnp.float32, least / len(cuts), top_value / len(cuts))
        return jnp.repeat(jnp.exp(draws), extent[position] // parts).reshape((-1,) + (1,) * (len(extent) - position - 1))

    factor_of = one(*cuts[0])
    for cut in cuts[1:]:
        factor_of = factor_of * one(*cut)
    return factor_of


def gaussian(stream_key, shape, width, limit, pieces=(), kind=jnp.bfloat16):
    entries = width * jax.random.normal(stream_key, shape, jnp.float32)
    if pieces:
        entries = entries * levels(stream_key, shape, pieces, -0.22, 0.18)
    return jnp.clip(entries, -limit, limit).astype(kind)


def setup_inputs(seed: int = 0) -> dict:
    streams_of = jax.random.split(jax.random.key(seed), 8)
    query_heads = draw_query_heads(jax.random.fold_in(streams_of[7], 71), 0)
    key_heads = draw_key_heads(jax.random.fold_in(streams_of[7], 71), 0)
    value_heads = gaussian(streams_of[2], (ALLROWS, INNER), 2.0, 12.0, ((0, 48), (1, 16)))
    modality = draw_modality(jax.random.fold_in(streams_of[7], 71), 0)
    doc_ids = draw_doc_ids(jax.random.fold_in(streams_of[7], 71), 0)
    out_weight = gaussian(streams_of[5], (2, INNER, D), (INNER // 4) ** -0.5, 0.1875, ((1, 16),))
    out_grad = gaussian(streams_of[6], (ALLROWS, D), 1.0, 6.0, ((0, 48),))
    return {"query_heads": query_heads, "key_heads": key_heads, "value_heads": value_heads, "modality": modality, "doc_ids": doc_ids, "out_weight": out_weight, "out_grad": out_grad}


MASKED = -1.0e30


def rounded(array):
    return lax.optimization_barrier(array.astype(jnp.bfloat16)).astype(jnp.float32)


def slot_info(modal_row, doc_row, modal_side, row_count):
    pack_len = modal_row.shape[0]
    chosen = modal_row == modal_side
    slot_pos = jnp.nonzero(chosen, size=row_count, fill_value=pack_len - 1)[0].astype(jnp.int32)
    slot_doc = jnp.take(doc_row, slot_pos)
    live_slot = jnp.arange(row_count, dtype=jnp.int32) < jnp.sum(chosen.astype(jnp.int32))
    return slot_pos, slot_doc, live_slot


def allowed(query_info, key_info):
    before = key_info[0][None, :] <= query_info[0][:, None]
    same_doc = key_info[1][None, :] == query_info[1][:, None]
    return before & same_doc & key_info[2][None, :]


def pair_layer(packed):
    modal_row, doc_row, query_pair, key_pair, value_pair, grad_pair = packed
    row_count = query_pair.shape[1]
    text_info = slot_info(modal_row, doc_row, 0, row_count)
    image_info = slot_info(modal_row, doc_row, 1, row_count)
    joined = tuple(jnp.concatenate((text_part, image_part)) for text_part, image_part in zip(text_info, image_info))
    permit = allowed(joined, joined)
    shape3 = (2 * row_count, HEADS, HD)
    q_all = query_pair.reshape(shape3).astype(jnp.float32)
    k_all = key_pair.reshape(shape3).astype(jnp.float32)
    v_all = value_pair.reshape(shape3).astype(jnp.float32)
    grad_all = grad_pair.reshape(shape3).astype(jnp.float32)
    factor = HD ** -0.5
    highest = lax.Precision.HIGHEST
    scores = jnp.where(permit[None], jnp.einsum("qhd,khd->hqk", q_all, k_all, precision=highest) * factor, MASKED)
    top_score = jnp.max(scores, axis=2)
    weights = jnp.exp(scores - top_score[:, :, None])
    denominator = jnp.sum(weights, axis=2)
    log_total = top_score + jnp.log(denominator)
    mixed = jnp.einsum("hqk,khd->qhd", rounded(weights), v_all, precision=highest)
    attended = (mixed / jnp.transpose(denominator)[:, :, None]).astype(jnp.bfloat16)
    delta_row = jnp.transpose(jnp.sum(grad_all * attended.astype(jnp.float32), axis=2))
    probability = jnp.exp(scores - log_total[:, :, None])
    grad_prob = jnp.einsum("qhd,khd->hqk", grad_all, v_all, precision=highest)
    dscore = rounded(probability * (grad_prob - delta_row[:, :, None]))
    grad_q = jnp.einsum("hqk,khd->qhd", dscore, k_all, precision=highest) * factor
    grad_k = jnp.einsum("hqk,qhd->khd", dscore, q_all, precision=highest) * factor
    grad_v = jnp.einsum("hqk,qhd->khd", rounded(probability), grad_all, precision=highest)
    out_shape = (2, row_count, HEADS * HD)
    return (attended.reshape(out_shape), grad_q.astype(jnp.bfloat16).reshape(out_shape),
            grad_k.astype(jnp.bfloat16).reshape(out_shape), grad_v.astype(jnp.bfloat16).reshape(out_shape))


def reference(query_heads, key_heads, value_heads, modality, doc_ids, out_weight, out_grad):
    pair_count = N_GRP // 2
    half_rows = pair_count * ROWS
    grad_parts = []
    for modal_side in range(2):
        grad_rows = out_grad[modal_side * half_rows:(modal_side + 1) * half_rows]
        grad_parts.append(lax.dot_general(grad_rows, out_weight[modal_side], (((1,), (1,)), ((), ())),
                                          preferred_element_type=jnp.float32).astype(jnp.bfloat16))
    grad_attended = jnp.concatenate(grad_parts)

    def by_pair(array):
        return jnp.swapaxes(array.reshape(2, pair_count, ROWS, array.shape[1]), 0, 1)

    def from_pair(array):
        return jnp.swapaxes(array, 0, 1).reshape(2 * half_rows, array.shape[3])

    packed = (modality[:pair_count], doc_ids[:pair_count], by_pair(query_heads), by_pair(key_heads),
              by_pair(value_heads), by_pair(grad_attended))
    attended, grad_query, grad_key, grad_value = lax.map(pair_layer, packed)
    attended = from_pair(attended)
    out_parts = []
    for modal_side in range(2):
        rows_here = attended[modal_side * half_rows:(modal_side + 1) * half_rows]
        out_parts.append(jnp.dot(rows_here, out_weight[modal_side], preferred_element_type=jnp.float32).astype(jnp.bfloat16))
    layer_output = jnp.concatenate(out_parts)
    return layer_output, from_pair(grad_query), from_pair(grad_key), from_pair(grad_value)
```

```python
import jax
import jax.numpy as jnp
from jax import lax
from jax.experimental import pallas as pl
from jax.experimental.pallas import tpu as pltpu
from jax.sharding import Mesh, PartitionSpec as P

HD = 128
MASKED = -1e30
FAR = 1e6
BF = jnp.bfloat16
F32 = jnp.float32
VMEM = pl.BlockSpec(memory_space=pltpu.VMEM)
SMEM = pl.BlockSpec(memory_space=pltpu.SMEM)
NT = (((1,), (1,)), ((), ()))
TN = (((0,), (0,)), ((), ()))


def cost(flops, nbytes, exps=0):
    return pl.CostEstimate(flops=flops, bytes_accessed=nbytes, transcendentals=exps)


def mask_body(side_ref, modal_ref, doc_ref, q_ref, k_ref):
    pack = modal_ref.shape[1]
    rows = q_ref.shape[1]
    own = (modal_ref[...] == side_ref[0]).astype(F32)
    other = 1.0 - own
    row8 = lax.broadcasted_iota(jnp.int32, (8, pack), 0)
    both = jnp.where(row8 == 0, own, other).astype(BF)
    before = lax.broadcasted_iota(jnp.int32, (pack, pack), 0) <= lax.broadcasted_iota(
        jnp.int32, (pack, pack), 1
    )
    upto = jnp.where(before, 1.0, 0.0).astype(BF)
    ranks = jnp.dot(both, upto, preferred_element_type=F32)
    slot = lax.broadcasted_iota(jnp.int32, (rows, pack), 0).astype(F32)
    spot = lax.broadcasted_iota(jnp.int32, (128, pack), 1)
    line = lax.broadcasted_iota(jnp.int32, (128, pack), 0)
    docs = doc_ref[...]
    fields = jnp.where(
        line == 0, spot // 256, jnp.where(line == 1, spot % 256, jnp.where(line == 2, docs, 0))
    )
    fields = fields.astype(F32).astype(BF)

    def picked(chosen, rank):
        code = jnp.where(chosen > 0.5, rank - 1.0, -1.0)
        return jnp.where(slot == code, 1.0, 0.0).astype(BF)

    own_pick = picked(own, ranks[0:1])
    other_pick = picked(other, ranks[1:2])
    own_count = ranks[0:1, pack - 1 : pack]
    other_count = ranks[1:2, pack - 1 : pack]
    query_line = lax.dot_general(fields, own_pick, NT, preferred_element_type=F32)
    q_live = lax.broadcasted_iota(jnp.int32, (1, rows), 1).astype(F32) < own_count
    last_doc = docs[0:1, pack - 1 : pack].astype(F32)
    q_pos = jnp.where(q_live, query_line[0:1] * 256.0 + query_line[1:2], float(pack - 1))
    q_doc = jnp.where(q_live, query_line[2:3], last_doc)
    line8 = lax.broadcasted_iota(jnp.int32, (8, rows), 0)
    q_first = q_doc * 1024.0
    q_ref[...] = jnp.where(line8 == 0, q_first, q_first + q_pos)
    k_row = lax.broadcasted_iota(jnp.int32, (rows, 1), 0).astype(F32)
    for part, (pick, count) in enumerate(((own_pick, own_count), (other_pick, other_count))):
        cols = lax.dot_general(pick, fields, NT, preferred_element_type=F32)
        code = cols[:, 2:3] * 1024.0 + cols[:, 0:1] * 256.0 + cols[:, 1:2]
        code = jnp.where(k_row < count, code, FAR)
        k_ref[part * rows : (part + 1) * rows, :] = jnp.broadcast_to(code, (rows, 128))


def slot_codes(side, modality, doc_ids, rows):
    pack = modality.shape[1]
    return pl.pallas_call(
        mask_body,
        out_shape=(
            jax.ShapeDtypeStruct((8, rows), F32),
            jax.ShapeDtypeStruct((2 * rows, 128), F32),
        ),
        in_specs=[SMEM, VMEM, VMEM],
        out_specs=(VMEM, VMEM),
        compiler_params=pltpu.CompilerParams(vmem_limit_bytes=12 * 1024 * 1024),
        cost_estimate=cost(4 * rows * pack * 128 * 2, 2 * rows * rows * 4),
        name="slot_codes",
    )(side, modality, doc_ids)


def weight_body(at_ref, weight_ref, grad_ref, *refs):
    slabs, out_ref, acc_ref = refs[:-2], refs[-2], refs[-1]
    step = pl.program_id(0)
    half = slabs[0].shape[0]
    part = lax.dot_general(grad_ref[...], weight_ref[0], NT, preferred_element_type=F32)
    mine = pl.ds(pl.multiple_of(at_ref[2] * half, half), half)
    for k, slab in enumerate(slabs):

        @pl.when(step == k)
        def _(slab=slab):
            slab[...] = weight_ref[0, mine, :]

    @pl.when(step == 0)
    def _():
        acc_ref[...] = part

    @pl.when(step > 0)
    def _():
        acc_ref[...] += part

    @pl.when(step == pl.num_programs(0) - 1)
    def _():
        out_ref[...] = acc_ref[...].astype(BF)


def weight_and_grad(at, out_weight, out_grad, slabs):
    _, cols, width = out_weight.shape
    rows = out_grad.shape[0]
    wide = width // slabs
    half = cols // 2
    return pl.pallas_call(
        weight_body,
        out_shape=(jax.ShapeDtypeStruct((half, wide), BF),) * slabs
        + (jax.ShapeDtypeStruct((rows, cols), BF),),
        grid_spec=pltpu.PrefetchScalarGridSpec(
            num_scalar_prefetch=1,
            grid=(slabs,),
            in_specs=[
                pl.BlockSpec((1, cols, wide), lambda i, at: (at[0], 0, (at[1] + i) % slabs)),
                pl.BlockSpec((rows, wide), lambda i, at: (0, (at[1] + i) % slabs)),
            ],
            out_specs=[pl.BlockSpec((half, wide), lambda i, at: (0, 0))] * slabs
            + [pl.BlockSpec((rows, cols), lambda i, at: (0, 0))],
            scratch_shapes=[pltpu.VMEM((rows, cols), F32)],
        ),
        compiler_params=pltpu.CompilerParams(
            dimension_semantics=("arbitrary",), vmem_limit_bytes=60 * 1024 * 1024
        ),
        cost_estimate=cost(2 * rows * cols * width, 2 * (2 * cols * width + rows * width)),
        name="weight_grad",
    )(at, out_weight, out_grad)


def scores(keys, q, key_code, query_code):
    s = lax.dot_general(keys, q, NT, preferred_element_type=F32) * (HD**-0.5)
    wide = jnp.concatenate([key_code] * (q.shape[0] // 128), axis=1)
    ok = (wide >= query_code[0:1]) & (wide <= query_code[1:2])
    return jnp.where(ok, s, MASKED)


def forward_body(
    q_ref, k_ref, v_ref, peer_ref, qc_ref, kc_ref, att_ref, copies_ref, total_ref
):
    rows, cols = q_ref.shape
    key_code = kc_ref[...]
    for h in range(cols // HD):
        c = slice(h * HD, (h + 1) * HD)
        keys = jnp.concatenate((k_ref[:, c], peer_ref[0, :, c]))
        values = jnp.concatenate((v_ref[:, c], peer_ref[1, :, c]))
        for t in range(0, rows, 256):
            r = slice(t, t + 256)
            s = scores(keys, q_ref[r, c], key_code, qc_ref[:, r])
            top = jnp.max(s, axis=0, keepdims=True)
            w = jnp.exp(s - top)
            denominator = jnp.sum(w, axis=0, keepdims=True)
            total_ref[h, :, r] = jnp.broadcast_to(top + jnp.log(denominator), (8, 256))
            mixed = lax.dot_general(values, w.astype(BF), TN, preferred_element_type=F32)
            att = jnp.transpose(mixed / denominator).astype(BF)
            att_ref[r, c] = att
            for x in range(copies_ref.shape[0]):
                copies_ref[x, r, c] = att


def forward(q, k, v, peer, codes, copies):
    rows, cols = q.shape
    heads = cols // HD
    return pl.pallas_call(
        forward_body,
        out_shape=(
            jax.ShapeDtypeStruct((rows, cols), BF),
            jax.ShapeDtypeStruct((copies, rows, cols), BF),
            jax.ShapeDtypeStruct((heads, 8, rows), F32),
        ),
        in_specs=[VMEM] * 6,
        out_specs=(VMEM,) * 3,
        compiler_params=pltpu.CompilerParams(vmem_limit_bytes=20 * 1024 * 1024),
        cost_estimate=cost(
            8 * heads * rows * rows * HD, 12 * rows * rows * heads, 2 * heads * rows * rows
        ),
        name="attend",
    )(q, k, v, peer, *codes)


def backward_body(
    q_ref,
    k_ref,
    v_ref,
    peer_ref,
    ga_ref,
    att_ref,
    qc_ref,
    kc_ref,
    total_ref,
    dq_ref,
    own_ref,
    cross_ref,
):
    rows, cols = q_ref.shape
    factor = HD ** (-0.5)
    key_code = kc_ref[...]
    for h in range(cols // HD):
        c = slice(h * HD, (h + 1) * HD)
        keys = jnp.concatenate((k_ref[:, c], peer_ref[0, :, c]))
        values = jnp.concatenate((v_ref[:, c], peer_ref[1, :, c]))
        dk = jnp.zeros((2 * rows, HD), F32)
        dv = jnp.zeros((2 * rows, HD), F32)
        for t in range(0, rows, 256):
            r = slice(t, t + 256)
            ga = ga_ref[r, c]
            q = q_ref[r, c]
            both = ga.astype(F32) * att_ref[r, c].astype(F32)
            delta = jnp.sum(jnp.transpose(both), axis=0, keepdims=True)
            s = scores(keys, q, key_code, qc_ref[:, r])
            prob = jnp.exp(s - total_ref[h, 0:1, r])
            dp = lax.dot_general(values, ga, NT, preferred_element_type=F32)
            ds = (prob * (dp - delta)).astype(BF)
            dq = lax.dot_general(keys, ds, TN, preferred_element_type=F32)
            dq_ref[r, c] = jnp.transpose(dq * factor).astype(BF)
            dk = dk + jnp.dot(ds, q, preferred_element_type=F32)
            dv = dv + jnp.dot(prob.astype(BF), ga, preferred_element_type=F32)
        dk = dk * factor
        own_ref[0, :, c] = dk[:rows]
        own_ref[1, :, c] = dv[:rows]
        cross_ref[0, :, c] = dk[rows:].astype(BF)
        cross_ref[1, :, c] = dv[rows:].astype(BF)


def backward(q, k, v, peer, ga, att, codes, total):
    rows, cols = q.shape
    heads = cols // HD
    return pl.pallas_call(
        backward_body,
        out_shape=(
            jax.ShapeDtypeStruct((rows, cols), BF),
            jax.ShapeDtypeStruct((2, rows, cols), F32),
            jax.ShapeDtypeStruct((2, rows, cols), BF),
        ),
        in_specs=[VMEM] * 9,
        out_specs=(VMEM,) * 3,
        compiler_params=pltpu.CompilerParams(vmem_limit_bytes=20 * 1024 * 1024),
        cost_estimate=cost(
            20 * heads * rows * rows * HD, 12 * rows * rows * heads, 2 * heads * rows * rows
        ),
        name="attend_back",
    )(q, k, v, peer, ga, att, *codes, total)


def project_body(at_ref, att_ref, mine_ref, other_ref, out_ref):
    parts, rows, cols = att_ref.shape
    half = cols // 2
    mine = pl.ds(pl.multiple_of(at_ref[2] * half, half), half)
    other = pl.ds(pl.multiple_of((1 - at_ref[2]) * half, half), half)
    lhs = []
    for k in range(parts):
        source = (at_ref[1] + parts - k) % parts
        lhs.append(jnp.concatenate((att_ref[source, :, mine], att_ref[source, :, other]), axis=1))
    for n in range(out_ref.shape[0]):
        c = slice(n * cols, (n + 1) * cols)
        total = jnp.zeros((rows, cols), F32)
        for k in range(parts):
            rhs = jnp.concatenate((mine_ref[k, :, c], other_ref[k, :, c]), axis=0)
            total = total + jnp.dot(lhs[k], rhs, preferred_element_type=F32)
        out_ref[n] = total.astype(BF)


def project(at, att, mine, other):
    parts, rows, cols = att.shape
    outs = mine.shape[2] // cols
    return pl.pallas_call(
        project_body,
        out_shape=jax.ShapeDtypeStruct((outs, rows, cols), BF),
        in_specs=[SMEM] + [VMEM] * 3,
        out_specs=VMEM,
        compiler_params=pltpu.CompilerParams(vmem_limit_bytes=12 * 1024 * 1024),
        cost_estimate=cost(2 * parts * rows * cols * outs * cols, 4 * mine.size + 4 * att.size),
        name="project",
    )(at, att, mine, other)


def step(query_heads, key_heads, value_heads, modality, doc_ids, out_weight, out_grad):
    rows, _ = query_heads.shape
    at = jnp.stack([lax.axis_index(a).astype(jnp.int32) for a in ("side", "x", "core")])
    swap = [(0, 1), (1, 0)]
    xs = lax.axis_size("x")
    peer = lax.ppermute(jnp.stack((key_heads, value_heads)), "side", swap)
    *slabs, grad_attended = weight_and_grad(at, out_weight, out_grad, xs)
    mine = [slabs[0]]
    for k in range(1, xs):
        mine.append(lax.ppermute(slabs[k], "x", [(i, (i + k) % xs) for i in range(xs)]))
    modality, _ = lax.optimization_barrier((modality, grad_attended))
    codes = slot_codes(at, modality, doc_ids, rows)
    attended, spread, total = forward(query_heads, key_heads, value_heads, peer, codes, xs)
    gathered = lax.all_to_all(spread, "x", 0, 0, tiled=True)
    mine = jnp.stack(mine)
    other = lax.ppermute(mine, "core", swap)
    grad_query, own, cross = backward(
        query_heads, key_heads, value_heads, peer, grad_attended, attended, codes, total
    )
    returned = lax.ppermute(cross, "side", swap)
    partial = project(at, gathered, mine, other)
    pieces = lax.all_to_all(partial, "y", 0, 0, tiled=True)
    layer_output = jnp.sum(pieces.astype(F32), axis=0).astype(BF)
    grad_key = (own[0] + returned[0].astype(F32)).astype(BF)
    grad_value = (own[1] + returned[1].astype(F32)).astype(BF)
    return (layer_output, grad_query, grad_key, grad_value)


def solution(mesh):
    groups, _ = mesh.devices.shape
    split = Mesh(mesh.devices.reshape(2, groups // 4, 2, 4, 4), ("side", "z", "core", "x", "y"))
    grp, tp = ("side", "z", "core"), ("x", "y")
    tokens = P(grp, tp)
    placed = (
        tokens,
        tokens,
        tokens,
        P(grp, None),
        P(grp, None),
        P(None, tp, None),
        P(grp, None),
    )
    return jax.shard_map(
        step,
        mesh=split,
        in_specs=placed,
        out_specs=(tokens, tokens, tokens, tokens),
        check_vma=False,
    )
```

```python
import jax
import jax.numpy as jnp
from jax import lax
from jax.experimental import pallas as pl
from jax.experimental.pallas import tpu as pltpu
from jax.sharding import Mesh, PartitionSpec as P

HD = 128
MASKED = -1e30
FAR = 1e6
BF = jnp.bfloat16
F32 = jnp.float32
VMEM = pl.BlockSpec(memory_space=pltpu.VMEM)
SMEM = pl.BlockSpec(memory_space=pltpu.SMEM)
HBM = pl.BlockSpec(memory_space=pltpu.HBM)
NT = (((1,), (1,)), ((), ()))
TN = (((0,), (0,)), ((), ()))


def cost(flops, nbytes, exps=0):
    return pl.CostEstimate(flops=flops, bytes_accessed=nbytes, transcendentals=exps)


def mask_body(side_ref, modal_ref, doc_ref, q_ref, k_ref, kept_ref, sem):
    pack = modal_ref.shape[1]
    rows = q_ref.shape[1]
    own = (modal_ref[...] == side_ref[0]).astype(F32)
    other = 1.0 - own
    row8 = lax.broadcasted_iota(jnp.int32, (8, pack), 0)
    both = jnp.where(row8 == 0, own, other).astype(BF)
    before = lax.broadcasted_iota(jnp.int32, (pack, pack), 0) <= lax.broadcasted_iota(
        jnp.int32, (pack, pack), 1
    )
    upto = jnp.where(before, 1.0, 0.0).astype(BF)
    ranks = jnp.dot(both, upto, preferred_element_type=F32)
    slot = lax.broadcasted_iota(jnp.int32, (rows, pack), 0).astype(F32)
    spot = lax.broadcasted_iota(jnp.int32, (128, pack), 1)
    line = lax.broadcasted_iota(jnp.int32, (128, pack), 0)
    docs = doc_ref[...]
    fields = jnp.where(
        line == 0, spot // 256, jnp.where(line == 1, spot % 256, jnp.where(line == 2, docs, 0))
    )
    fields = fields.astype(F32).astype(BF)

    def picked(chosen, rank):
        code = jnp.where(chosen > 0.5, rank - 1.0, -1.0)
        return jnp.where(slot == code, 1.0, 0.0).astype(BF)

    own_pick = picked(own, ranks[0:1])
    other_pick = picked(other, ranks[1:2])
    own_count = ranks[0:1, pack - 1 : pack]
    other_count = ranks[1:2, pack - 1 : pack]
    query_line = lax.dot_general(fields, own_pick, NT, preferred_element_type=F32)
    q_live = lax.broadcasted_iota(jnp.int32, (1, rows), 1).astype(F32) < own_count
    last_doc = docs[0:1, pack - 1 : pack].astype(F32)
    q_pos = jnp.where(q_live, query_line[0:1] * 256.0 + query_line[1:2], float(pack - 1))
    q_doc = jnp.where(q_live, query_line[2:3], last_doc)
    line8 = lax.broadcasted_iota(jnp.int32, (8, rows), 0)
    q_first = q_doc * 1024.0
    q_ref[...] = jnp.where(line8 == 0, q_first, q_first + q_pos)
    k_row = lax.broadcasted_iota(jnp.int32, (rows, 1), 0).astype(F32)
    for part, (pick, count) in enumerate(((own_pick, own_count), (other_pick, other_count))):
        cols = lax.dot_general(pick, fields, NT, preferred_element_type=F32)
        code = cols[:, 2:3] * 1024.0 + cols[:, 0:1] * 256.0 + cols[:, 1:2]
        code = jnp.where(k_row < count, code, FAR)
        k_ref[part * rows : (part + 1) * rows, :] = jnp.broadcast_to(code, (rows, 128))
    keep = pltpu.make_async_copy(k_ref, kept_ref, sem)
    keep.start()
    keep.wait()


def slot_codes(side, modality, doc_ids, rows):
    pack = modality.shape[1]
    return pl.pallas_call(
        mask_body,
        out_shape=(
            jax.ShapeDtypeStruct((8, rows), F32),
            jax.ShapeDtypeStruct((2 * rows, 128), F32),
            jax.ShapeDtypeStruct((2 * rows, 128), F32),
        ),
        in_specs=[SMEM, VMEM, VMEM],
        out_specs=(VMEM, VMEM, HBM),
        scratch_shapes=[pltpu.SemaphoreType.DMA],
        compiler_params=pltpu.CompilerParams(vmem_limit_bytes=12 * 1024 * 1024),
        cost_estimate=cost(4 * rows * pack * 128 * 2, 2 * rows * rows * 4),
        name="slot_codes",
    )(side, modality, doc_ids)


def slab_body(at_ref, weight_ref, slab_ref, sems):
    parts, half, wide = slab_ref.shape
    mine = pl.ds(pl.multiple_of(at_ref[2] * half, half), half)
    copies = [
        pltpu.make_async_copy(
            weight_ref.at[at_ref[0], mine, pl.ds(i * wide, wide)], slab_ref.at[i], sems.at[i]
        )
        for i in range(parts)
    ]
    for copy in copies:
        copy.start()
    for copy in copies:
        copy.wait()


def weight_slabs(at, out_weight, parts):
    _, cols, width = out_weight.shape
    shape = (parts, cols // 2, width // parts)
    return pl.pallas_call(
        slab_body,
        out_shape=jax.ShapeDtypeStruct(shape, BF),
        in_specs=[SMEM, HBM],
        out_specs=VMEM,
        scratch_shapes=[pltpu.SemaphoreType.DMA((parts,))],
        compiler_params=pltpu.CompilerParams(vmem_limit_bytes=60 * 1024 * 1024),
        cost_estimate=cost(0, 2 * cols * width),
        name="weight_slabs",
    )(at, out_weight)


GRAD_STEPS = 8


def grad_body(at_ref, weight_ref, grad_ref, out_ref, w_buf, g_buf, sems):
    wide = w_buf.shape[1] // GRAD_STEPS
    copies = []
    for i in range(GRAD_STEPS):
        c = pl.ds(i * wide, wide)
        for n, (src, dst) in enumerate(
            ((weight_ref.at[at_ref[0], :, c], w_buf), (grad_ref.at[:, c], g_buf))
        ):
            copy = pltpu.make_async_copy(src, dst.at[:, c], sems.at[n, i])
            copy.start()
            copies.append(copy)
    total = jnp.zeros(out_ref.shape, F32)
    for i in range(GRAD_STEPS):
        copies[2 * i].wait()
        copies[2 * i + 1].wait()
        c = slice(i * wide, (i + 1) * wide)
        total = total + lax.dot_general(
            g_buf[:, c], w_buf[:, c], NT, preferred_element_type=F32
        )
    out_ref[...] = total.astype(BF)


def attended_grad(at, out_weight, out_grad):
    _, cols, width = out_weight.shape
    rows = out_grad.shape[0]
    return pl.pallas_call(
        grad_body,
        out_shape=jax.ShapeDtypeStruct((rows, cols), BF),
        in_specs=[SMEM, HBM, HBM],
        out_specs=VMEM,
        scratch_shapes=[
            pltpu.VMEM((cols, width), BF),
            pltpu.VMEM((rows, width), BF),
            pltpu.SemaphoreType.DMA((2, GRAD_STEPS)),
        ],
        compiler_params=pltpu.CompilerParams(vmem_limit_bytes=60 * 1024 * 1024),
        cost_estimate=cost(2 * rows * cols * width, 2 * (cols + rows) * width),
        name="attended_grad",
    )(at, out_weight, out_grad)


def scores(keys, q, key_code, query_code):
    s = lax.dot_general(keys, q, NT, preferred_element_type=F32) * (HD**-0.5)
    wide = jnp.concatenate([key_code] * (q.shape[0] // 128), axis=1)
    ok = (wide >= query_code[0:1]) & (wide <= query_code[1:2])
    return jnp.where(ok, s, MASKED)


def forward_body(q_ref, k_ref, v_ref, peer_ref, qc_ref, kc_ref, copies_ref, total_ref):
    rows, cols = q_ref.shape
    key_code = kc_ref[...]
    for h in range(cols // HD):
        c = slice(h * HD, (h + 1) * HD)
        keys = jnp.concatenate((k_ref[:, c], peer_ref[0, :, c]))
        values = jnp.concatenate((v_ref[:, c], peer_ref[1, :, c]))
        for t in range(0, rows, 256):
            r = slice(t, t + 256)
            s = scores(keys, q_ref[r, c], key_code, qc_ref[:, r])
            top = jnp.max(s, axis=0, keepdims=True)
            w = jnp.exp(s - top)
            denominator = jnp.sum(w, axis=0, keepdims=True)
            total_ref[h, :, r] = jnp.broadcast_to(top + jnp.log(denominator), (8, 256))
            mixed = lax.dot_general(values, w.astype(BF), TN, preferred_element_type=F32)
            att = jnp.transpose(mixed / denominator).astype(BF)
            for x in range(copies_ref.shape[0]):
                copies_ref[x, r, c] = att


def forward(q, k, v, peer, codes, copies):
    rows, cols = q.shape
    heads = cols // HD
    return pl.pallas_call(
        forward_body,
        out_shape=(
            jax.ShapeDtypeStruct((copies, rows, cols), BF),
            jax.ShapeDtypeStruct((heads, 8, rows), F32),
        ),
        in_specs=[VMEM] * 6,
        out_specs=(VMEM,) * 2,
        compiler_params=pltpu.CompilerParams(vmem_limit_bytes=20 * 1024 * 1024),
        cost_estimate=cost(
            8 * heads * rows * rows * HD, 12 * rows * rows * heads, 2 * heads * rows * rows
        ),
        name="attend",
    )(q, k, v, peer, *codes)


def backward_body(
    q_hbm,
    k_hbm,
    v_hbm,
    peer_hbm,
    ga_hbm,
    spread_hbm,
    kc_hbm,
    qc_ref,
    total_ref,
    dq_ref,
    own_ref,
    cross_ref,
    q_ref,
    k_ref,
    v_ref,
    peer_ref,
    ga_ref,
    att_ref,
    kc_ref,
    sems,
):
    sources = (kc_hbm, q_hbm, k_hbm, peer_hbm, ga_hbm, v_hbm, spread_hbm.at[0])
    targets = (kc_ref, q_ref, k_ref, peer_ref, ga_ref, v_ref, att_ref)
    loads = [
        pltpu.make_async_copy(src, dst, sems.at[n])
        for n, (src, dst) in enumerate(zip(sources, targets))
    ]
    for load in loads:
        load.start()
    for load in loads:
        load.wait()
    rows, cols = q_ref.shape
    factor = HD ** (-0.5)
    key_code = kc_ref[...]
    for h in range(cols // HD):
        c = slice(h * HD, (h + 1) * HD)
        keys = jnp.concatenate((k_ref[:, c], peer_ref[0, :, c]))
        values = jnp.concatenate((v_ref[:, c], peer_ref[1, :, c]))
        dk = jnp.zeros((2 * rows, HD), F32)
        dv = jnp.zeros((2 * rows, HD), F32)
        for t in range(0, rows, 256):
            r = slice(t, t + 256)
            ga = ga_ref[r, c]
            q = q_ref[r, c]
            both = ga.astype(F32) * att_ref[r, c].astype(F32)
            delta = jnp.sum(jnp.transpose(both), axis=0, keepdims=True)
            s = scores(keys, q, key_code, qc_ref[:, r])
            prob = jnp.exp(s - total_ref[h, 0:1, r])
            dp = lax.dot_general(values, ga, NT, preferred_element_type=F32)
            ds = (prob * (dp - delta)).astype(BF)
            dq = lax.dot_general(keys, ds, TN, preferred_element_type=F32)
            dq_ref[r, c] = jnp.transpose(dq * factor).astype(BF)
            dk = dk + jnp.dot(ds, q, preferred_element_type=F32)
            dv = dv + jnp.dot(prob.astype(BF), ga, preferred_element_type=F32)
        dk = dk * factor
        own_ref[0, :, c] = dk[:rows]
        own_ref[1, :, c] = dv[:rows]
        cross_ref[0, :, c] = dk[rows:].astype(BF)
        cross_ref[1, :, c] = dv[rows:].astype(BF)


def backward(q, k, v, peer, ga, spread, kept, query_code, total):
    rows, cols = q.shape
    heads = cols // HD
    return pl.pallas_call(
        backward_body,
        out_shape=(
            jax.ShapeDtypeStruct((rows, cols), BF),
            jax.ShapeDtypeStruct((2, rows, cols), F32),
            jax.ShapeDtypeStruct((2, rows, cols), BF),
        ),
        in_specs=[HBM] * 7 + [VMEM] * 2,
        out_specs=(VMEM,) * 3,
        scratch_shapes=[
            pltpu.VMEM((rows, cols), BF),
            pltpu.VMEM((rows, cols), BF),
            pltpu.VMEM((rows, cols), BF),
            pltpu.VMEM((2, rows, cols), BF),
            pltpu.VMEM((rows, cols), BF),
            pltpu.VMEM((rows, cols), BF),
            pltpu.VMEM((2 * rows, 128), F32),
            pltpu.SemaphoreType.DMA((7,)),
        ],
        compiler_params=pltpu.CompilerParams(vmem_limit_bytes=60 * 1024 * 1024),
        cost_estimate=cost(
            20 * heads * rows * rows * HD, 12 * rows * rows * heads, 2 * heads * rows * rows
        ),
        name="attend_back",
    )(q, k, v, peer, ga, spread, kept, query_code, total)


def project_body(at_ref, att_ref, mine_ref, other_ref, out_ref):
    parts, rows, cols = att_ref.shape
    half = cols // 2
    lhs = []
    for which in (at_ref[2], 1 - at_ref[2]):
        lanes = pl.ds(pl.multiple_of(which * half, half), half)
        lhs.append(jnp.concatenate([att_ref[x, :, lanes] for x in range(parts)], axis=1))
    for n in range(out_ref.shape[0]):
        c = slice(n * cols, (n + 1) * cols)
        total = jnp.zeros((rows, cols), F32)
        for left, right in zip(lhs, (mine_ref, other_ref)):
            right = jnp.concatenate([right[x, :, c] for x in range(parts)], axis=0)
            total = total + jnp.dot(left, right, preferred_element_type=F32)
        out_ref[n] = total.astype(BF)


def project(at, att, mine, other):
    parts, rows, cols = att.shape
    outs = mine.shape[2] // cols
    return pl.pallas_call(
        project_body,
        out_shape=jax.ShapeDtypeStruct((outs, rows, cols), BF),
        in_specs=[SMEM] + [VMEM] * 3,
        out_specs=VMEM,
        compiler_params=pltpu.CompilerParams(vmem_limit_bytes=12 * 1024 * 1024),
        cost_estimate=cost(2 * parts * rows * cols * outs * cols, 4 * mine.size + 4 * att.size),
        name="project",
    )(at, att, mine, other)


def step(query_heads, key_heads, value_heads, modality, doc_ids, out_weight, out_grad):
    rows, _ = query_heads.shape
    at = jnp.stack([lax.axis_index(a).astype(jnp.int32) for a in ("side", "x", "core")])
    swap = [(0, 1), (1, 0)]
    xs = lax.axis_size("x")
    peer = lax.ppermute(jnp.stack((key_heads, value_heads)), "side", swap)
    slabs = weight_slabs(at, out_weight, xs)
    mine = lax.all_to_all(slabs, "x", 0, 0, tiled=True)
    modality, _ = lax.optimization_barrier((modality, slabs))
    query_code, key_code, kept = slot_codes(at, modality, doc_ids, rows)
    out_grad, _ = lax.optimization_barrier((out_grad, query_code))
    grad_attended = attended_grad(at, out_weight, out_grad)
    spread, total = forward(query_heads, key_heads, value_heads, peer, (query_code, key_code), xs)
    gathered = lax.all_to_all(spread, "x", 0, 0, tiled=True)
    other = lax.ppermute(mine, "core", swap)
    grad_query, own, cross = backward(
        query_heads,
        key_heads,
        value_heads,
        peer,
        grad_attended,
        spread,
        kept,
        query_code,
        total,
    )
    returned = lax.ppermute(cross, "side", swap)
    partial = project(at, gathered, mine, other)
    pieces = lax.all_to_all(partial, "y", 0, 0, tiled=True)
    layer_output = jnp.sum(pieces.astype(F32), axis=0).astype(BF)
    grad_key = (own[0] + returned[0].astype(F32)).astype(BF)
    grad_value = (own[1] + returned[1].astype(F32)).astype(BF)
    return (layer_output, grad_query, grad_key, grad_value)


def solution(mesh):
    groups, _ = mesh.devices.shape
    split = Mesh(mesh.devices.reshape(2, groups // 4, 2, 4, 4), ("side", "z", "core", "x", "y"))
    grp, tp = ("side", "z", "core"), ("x", "y")
    tokens = P(grp, tp)
    placed = (
        tokens,
        tokens,
        tokens,
        P(grp, None),
        P(grp, None),
        P(None, tp, None),
        P(grp, None),
    )
    return jax.shard_map(
        step,
        mesh=split,
        in_specs=placed,
        out_specs=(tokens, tokens, tokens, tokens),
        check_vma=False,
    )
```

```python
import jax
import jax.numpy as jnp
from jax import lax
from jax.experimental import pallas as pl
from jax.experimental.pallas import tpu as pltpu
from jax.sharding import Mesh, PartitionSpec as P

HD = 128
MASKED = -1e30
FAR = 1e6
BF = jnp.bfloat16
F32 = jnp.float32
VMEM = pl.BlockSpec(memory_space=pltpu.VMEM)
SMEM = pl.BlockSpec(memory_space=pltpu.SMEM)
HBM = pl.BlockSpec(memory_space=pltpu.HBM)
NT = (((1,), (1,)), ((), ()))
TN = (((0,), (0,)), ((), ()))


def cost(flops, nbytes, exps=0):
    return pl.CostEstimate(flops=flops, bytes_accessed=nbytes, transcendentals=exps)


def codes_into(side, modal_ref, doc_ref, q_ref, k_ref):
    pack = modal_ref.shape[1]
    rows = q_ref.shape[1]
    own = (modal_ref[...] == side).astype(F32)
    other = 1.0 - own
    row8 = lax.broadcasted_iota(jnp.int32, (8, pack), 0)
    both = jnp.where(row8 == 0, own, other).astype(BF)
    before = lax.broadcasted_iota(jnp.int32, (pack, pack), 0) <= lax.broadcasted_iota(
        jnp.int32, (pack, pack), 1
    )
    upto = jnp.where(before, 1.0, 0.0).astype(BF)
    ranks = jnp.dot(both, upto, preferred_element_type=F32)
    slot = lax.broadcasted_iota(jnp.int32, (rows, pack), 0).astype(F32)
    spot = lax.broadcasted_iota(jnp.int32, (128, pack), 1)
    line = lax.broadcasted_iota(jnp.int32, (128, pack), 0)
    docs = doc_ref[...]
    fields = jnp.where(
        line == 0, spot // 256, jnp.where(line == 1, spot % 256, jnp.where(line == 2, docs, 0))
    )
    fields = fields.astype(F32).astype(BF)

    def picked(chosen, rank):
        code = jnp.where(chosen > 0.5, rank - 1.0, -1.0)
        return jnp.where(slot == code, 1.0, 0.0).astype(BF)

    own_pick = picked(own, ranks[0:1])
    other_pick = picked(other, ranks[1:2])
    own_count = ranks[0:1, pack - 1 : pack]
    other_count = ranks[1:2, pack - 1 : pack]
    query_line = lax.dot_general(fields, own_pick, NT, preferred_element_type=F32)
    q_live = lax.broadcasted_iota(jnp.int32, (1, rows), 1).astype(F32) < own_count
    last_doc = docs[0:1, pack - 1 : pack].astype(F32)
    q_pos = jnp.where(q_live, query_line[0:1] * 256.0 + query_line[1:2], float(pack - 1))
    q_doc = jnp.where(q_live, query_line[2:3], last_doc)
    line8 = lax.broadcasted_iota(jnp.int32, (8, rows), 0)
    q_first = q_doc * 1024.0
    q_ref[...] = jnp.where(line8 == 0, q_first, q_first + q_pos)
    k_row = lax.broadcasted_iota(jnp.int32, (rows, 1), 0).astype(F32)
    for part, (pick, count) in enumerate(((own_pick, own_count), (other_pick, other_count))):
        cols = lax.dot_general(pick, fields, NT, preferred_element_type=F32)
        code = cols[:, 2:3] * 1024.0 + cols[:, 0:1] * 256.0 + cols[:, 1:2]
        code = jnp.where(k_row < count, code, FAR)
        k_ref[part * rows : (part + 1) * rows, :] = jnp.broadcast_to(code, (rows, 128))


def slab_body(at_ref, weight_ref, slab_ref, buf_ref, sems):
    parts, half, wide = slab_ref.shape
    mine = pl.ds(pl.multiple_of(at_ref[2] * half, half), half)
    loads, saves = [], []
    for i in range(parts):
        source = weight_ref.at[at_ref[0], mine, pl.ds(i * wide, wide)]
        loads.append(pltpu.make_async_copy(source, buf_ref.at[i], sems.at[0, i]))
        saves.append(pltpu.make_async_copy(buf_ref.at[i], slab_ref.at[i], sems.at[1, i]))
    for load in loads:
        load.start()
    for load, save in zip(loads, saves):
        load.wait()
        save.start()
    for save in saves:
        save.wait()


def weight_slabs(at, out_weight, parts):
    _, cols, width = out_weight.shape
    shape = (parts, cols // 2, width // parts)
    return pl.pallas_call(
        slab_body,
        out_shape=jax.ShapeDtypeStruct(shape, BF),
        in_specs=[SMEM, HBM],
        out_specs=HBM,
        scratch_shapes=[pltpu.VMEM(shape, BF), pltpu.SemaphoreType.DMA((2, parts))],
        compiler_params=pltpu.CompilerParams(vmem_limit_bytes=60 * 1024 * 1024),
        cost_estimate=cost(0, 2 * cols * width),
        name="weight_slabs",
    )(at, out_weight)


GRAD_STEPS = 8


def prepare_body(
    at_ref, modal_ref, doc_ref, weight_ref, grad_ref, q_ref, k_ref, out_ref, w_buf, g_buf, sems
):
    wide = w_buf.shape[1] // GRAD_STEPS
    copies = []
    for i in range(GRAD_STEPS):
        c = pl.ds(i * wide, wide)
        for n, (src, dst) in enumerate(
            ((weight_ref.at[at_ref[0], :, c], w_buf), (grad_ref.at[:, c], g_buf))
        ):
            copy = pltpu.make_async_copy(src, dst.at[:, c], sems.at[n, i])
            copy.start()
            copies.append(copy)
    codes_into(at_ref[0], modal_ref, doc_ref, q_ref, k_ref)
    total = jnp.zeros(out_ref.shape, F32)
    for i in range(GRAD_STEPS):
        copies[2 * i].wait()
        copies[2 * i + 1].wait()
        c = slice(i * wide, (i + 1) * wide)
        total = total + lax.dot_general(
            g_buf[:, c], w_buf[:, c], NT, preferred_element_type=F32
        )
    out_ref[...] = total.astype(BF)


def prepare(at, modality, doc_ids, out_weight, out_grad):
    _, cols, width = out_weight.shape
    rows = out_grad.shape[0]
    return pl.pallas_call(
        prepare_body,
        out_shape=(
            jax.ShapeDtypeStruct((8, rows), F32),
            jax.ShapeDtypeStruct((2 * rows, 128), F32),
            jax.ShapeDtypeStruct((rows, cols), BF),
        ),
        in_specs=[SMEM, VMEM, VMEM, HBM, HBM],
        out_specs=(VMEM,) * 3,
        scratch_shapes=[
            pltpu.VMEM((cols, width), BF),
            pltpu.VMEM((rows, width), BF),
            pltpu.SemaphoreType.DMA((2, GRAD_STEPS)),
        ],
        compiler_params=pltpu.CompilerParams(vmem_limit_bytes=50 * 1024 * 1024),
        cost_estimate=cost(2 * rows * cols * width, 2 * (cols + rows) * width),
        name="prepare",
    )(at, modality, doc_ids, out_weight, out_grad)


def scores(keys, q, key_code, query_code):
    s = lax.dot_general(keys, q, NT, preferred_element_type=F32) * (HD**-0.5)
    wide = jnp.concatenate([key_code] * (q.shape[0] // 128), axis=1)
    ok = (wide >= query_code[0:1]) & (wide <= query_code[1:2])
    return jnp.where(ok, s, MASKED)


TILE = 256


def attention_body(
    q_ref,
    k_ref,
    v_ref,
    kp_ref,
    vp_ref,
    ga_ref,
    qc_ref,
    kc_ref,
    spread_ref,
    dq_ref,
    own_ref,
    cross_ref,
    w_buf,
    inv_buf,
    att_buf,
    dq_buf,
    own_buf,
    cross_buf,
    sems,
):
    rows, cols = q_ref.shape
    heads = cols // HD
    factor = HD ** (-0.5)
    key_code = kc_ref[...]
    lanes = [slice(h * HD, (h + 1) * HD) for h in range(heads)]
    keys = [jnp.concatenate((k_ref[:, c], kp_ref[:, c])) for c in lanes]
    values = [jnp.concatenate((v_ref[:, c], vp_ref[:, c])) for c in lanes]
    saves = []

    def save(src, dst):
        copy = pltpu.make_async_copy(src, dst, sems.at[len(saves)])
        copy.start()
        saves.append(copy)

    for h, c in enumerate(lanes):
        for t in range(0, rows, TILE):
            r = slice(t, t + TILE)
            s = scores(keys[h], q_ref[r, c], key_code, qc_ref[:, r])
            top = jnp.max(s, axis=0, keepdims=True)
            w = jnp.exp(s - top)
            w_buf[h, :, r] = w
            inv = 1.0 / jnp.sum(w, axis=0, keepdims=True)
            inv_buf[h, :, r] = jnp.broadcast_to(inv, (8, TILE))
            mixed = lax.dot_general(values[h], w.astype(BF), TN, preferred_element_type=F32)
            att_buf[r, c] = jnp.transpose(mixed * inv).astype(BF)
        for x in range(spread_ref.shape[0]):
            save(att_buf.at[:, c], spread_ref.at[x, :, c])
    for h, c in enumerate(lanes):
        dk = jnp.zeros((2 * rows, HD), F32)
        dv = jnp.zeros((2 * rows, HD), F32)
        for t in range(0, rows, TILE):
            r = slice(t, t + TILE)
            ga = ga_ref[r, c]
            both = ga.astype(F32) * att_buf[r, c].astype(F32)
            delta = jnp.sum(jnp.transpose(both), axis=0, keepdims=True)
            prob = w_buf[h, :, r] * inv_buf[h, 0:1, r]
            dp = lax.dot_general(values[h], ga, NT, preferred_element_type=F32)
            ds = (prob * (dp - delta)).astype(BF)
            dq = lax.dot_general(keys[h], ds, TN, preferred_element_type=F32)
            dq_buf[r, c] = jnp.transpose(dq * factor).astype(BF)
            dk = dk + jnp.dot(ds, q_ref[r, c], preferred_element_type=F32)
            dv = dv + jnp.dot(prob.astype(BF), ga, preferred_element_type=F32)
        dk = dk * factor
        for n, grad in enumerate((dk, dv)):
            own_buf[n, :, c] = grad[:rows].astype(BF)
            cross_buf[n, :, c] = grad[rows:].astype(BF)
        save(cross_buf.at[:, :, c], cross_ref.at[:, :, c])
        save(dq_buf.at[:, c], dq_ref.at[:, c])
        save(own_buf.at[:, :, c], own_ref.at[:, :, c])
    for copy in saves:
        copy.wait()


def attention(q, k, v, k_peer, v_peer, ga, codes, copies):
    rows, cols = q.shape
    heads = cols // HD
    outs = (
        jax.ShapeDtypeStruct((copies, rows, cols), BF),
        jax.ShapeDtypeStruct((rows, cols), BF),
        jax.ShapeDtypeStruct((2, rows, cols), BF),
        jax.ShapeDtypeStruct((2, rows, cols), BF),
    )
    return pl.pallas_call(
        attention_body,
        out_shape=outs,
        in_specs=[VMEM] * 8,
        out_specs=(HBM,) * 4,
        scratch_shapes=[
            pltpu.VMEM((heads, 2 * rows, rows), F32),
            pltpu.VMEM((heads, 8, rows), F32),
            pltpu.VMEM((rows, cols), BF),
            pltpu.VMEM((rows, cols), BF),
            pltpu.VMEM((2, rows, cols), BF),
            pltpu.VMEM((2, rows, cols), BF),
            pltpu.SemaphoreType.DMA((heads * (copies + 3),)),
        ],
        compiler_params=pltpu.CompilerParams(vmem_limit_bytes=28 * 1024 * 1024),
        cost_estimate=cost(
            24 * heads * rows * rows * HD, 12 * rows * rows * heads, 2 * heads * rows * rows
        ),
        name="attention",
    )(q, k, v, k_peer, v_peer, ga, *codes)


def project_body(at_ref, att_ref, mine_ref, other_ref, out_ref):
    parts, rows, cols = att_ref.shape
    half = cols // 2
    lhs = []
    for which in (at_ref[2], 1 - at_ref[2]):
        lanes = pl.ds(pl.multiple_of(which * half, half), half)
        lhs.append(jnp.concatenate([att_ref[x, :, lanes] for x in range(parts)], axis=1))
    for n in range(out_ref.shape[0]):
        c = slice(n * cols, (n + 1) * cols)
        total = jnp.zeros((rows, cols), F32)
        for left, right in zip(lhs, (mine_ref, other_ref)):
            right = jnp.concatenate([right[x, :, c] for x in range(parts)], axis=0)
            total = total + jnp.dot(left, right, preferred_element_type=F32)
        out_ref[n] = total.astype(BF)


def project(at, att, mine, other):
    parts, rows, cols = att.shape
    outs = mine.shape[2] // cols
    return pl.pallas_call(
        project_body,
        out_shape=jax.ShapeDtypeStruct((outs, rows, cols), BF),
        in_specs=[SMEM] + [VMEM] * 3,
        out_specs=VMEM,
        compiler_params=pltpu.CompilerParams(vmem_limit_bytes=12 * 1024 * 1024),
        cost_estimate=cost(2 * parts * rows * cols * outs * cols, 4 * mine.size + 4 * att.size),
        name="project",
    )(at, att, mine, other)


def finish_body(own_ref, back_ref, dk_ref, dv_ref):
    dk_ref[...] = (own_ref[0].astype(F32) + back_ref[0].astype(F32)).astype(BF)
    dv_ref[...] = (own_ref[1].astype(F32) + back_ref[1].astype(F32)).astype(BF)


def finish(own, back):
    shape = jax.ShapeDtypeStruct(own.shape[1:], BF)
    return pl.pallas_call(
        finish_body,
        out_shape=(shape, shape),
        in_specs=[VMEM] * 2,
        out_specs=(VMEM,) * 2,
        compiler_params=pltpu.CompilerParams(vmem_limit_bytes=60 * 1024 * 1024),
        cost_estimate=cost(own.size, 8 * own.size),
        name="finish",
    )(own, back)


def step(query_heads, key_heads, value_heads, modality, doc_ids, out_weight, out_grad):
    at = jnp.stack([lax.axis_index(a).astype(jnp.int32) for a in ("side", "x", "core")])
    swap = [(0, 1), (1, 0)]
    xs = lax.axis_size("x")
    k_peer = lax.ppermute(key_heads, "side", swap)
    v_peer = lax.ppermute(value_heads, "side", swap)
    slabs = weight_slabs(at, out_weight, xs)
    mine = lax.all_to_all(slabs, "x", 0, 0, tiled=True)
    modality, _ = lax.optimization_barrier((modality, slabs))
    query_code, key_code, grad_attended = prepare(
        at, modality, doc_ids, out_weight, out_grad
    )
    spread, grad_query, own, cross = attention(
        query_heads,
        key_heads,
        value_heads,
        k_peer,
        v_peer,
        grad_attended,
        (query_code, key_code),
        xs,
    )
    gathered = lax.all_to_all(spread, "x", 0, 0, tiled=True)
    other = lax.ppermute(mine, "core", swap)
    returned = lax.ppermute(cross, "side", swap)
    partial = project(at, gathered, mine, other)
    pieces = lax.all_to_all(partial, "y", 0, 0, tiled=True)
    layer_output = jnp.sum(pieces.astype(F32), axis=0).astype(BF)
    grad_key, grad_value = finish(own, returned)
    return (layer_output, grad_query, grad_key, grad_value)


def solution(mesh):
    groups, _ = mesh.devices.shape
    split = Mesh(mesh.devices.reshape(2, groups // 4, 2, 4, 4), ("side", "z", "core", "x", "y"))
    grp, tp = ("side", "z", "core"), ("x", "y")
    tokens = P(grp, tp)
    placed = (
        tokens,
        tokens,
        tokens,
        P(grp, None),
        P(grp, None),
        P(None, tp, None),
        P(grp, None),
    )
    return jax.shard_map(
        step,
        mesh=split,
        in_specs=placed,
        out_specs=(tokens, tokens, tokens, tokens),
        check_vma=False,
    )
```

```python
import jax
import jax.numpy as jnp
from jax import lax
from jax.experimental import pallas as pl
from jax.experimental.pallas import tpu as pltpu
from jax.sharding import Mesh, PartitionSpec as P

HD = 128
MASKED = -1e30
FAR = 1e6
BF = jnp.bfloat16
F32 = jnp.float32
VMEM = pl.BlockSpec(memory_space=pltpu.VMEM)
SMEM = pl.BlockSpec(memory_space=pltpu.SMEM)
HBM = pl.BlockSpec(memory_space=pltpu.HBM)
NT = (((1,), (1,)), ((), ()))
TN = (((0,), (0,)), ((), ()))


def cost(flops, nbytes, exps=0):
    return pl.CostEstimate(flops=flops, bytes_accessed=nbytes, transcendentals=exps)


def codes_into(side, modal_ref, doc_ref, q_ref, k_ref):
    pack = modal_ref.shape[1]
    rows = q_ref.shape[1]
    own = (modal_ref[...] == side).astype(F32)
    other = 1.0 - own
    row8 = lax.broadcasted_iota(jnp.int32, (8, pack), 0)
    both = jnp.where(row8 == 0, own, other).astype(BF)
    before = lax.broadcasted_iota(jnp.int32, (pack, pack), 0) <= lax.broadcasted_iota(
        jnp.int32, (pack, pack), 1
    )
    upto = jnp.where(before, 1.0, 0.0).astype(BF)
    ranks = jnp.dot(both, upto, preferred_element_type=F32)
    slot = lax.broadcasted_iota(jnp.int32, (rows, pack), 0).astype(F32)
    spot = lax.broadcasted_iota(jnp.int32, (128, pack), 1)
    line = lax.broadcasted_iota(jnp.int32, (128, pack), 0)
    docs = doc_ref[...]
    fields = jnp.where(
        line == 0, spot // 256, jnp.where(line == 1, spot % 256, jnp.where(line == 2, docs, 0))
    )
    fields = fields.astype(F32).astype(BF)

    def picked(chosen, rank):
        code = jnp.where(chosen > 0.5, rank - 1.0, -1.0)
        return jnp.where(slot == code, 1.0, 0.0).astype(BF)

    own_pick = picked(own, ranks[0:1])
    other_pick = picked(other, ranks[1:2])
    own_count = ranks[0:1, pack - 1 : pack]
    other_count = ranks[1:2, pack - 1 : pack]
    query_line = lax.dot_general(fields, own_pick, NT, preferred_element_type=F32)
    q_live = lax.broadcasted_iota(jnp.int32, (1, rows), 1).astype(F32) < own_count
    last_doc = docs[0:1, pack - 1 : pack].astype(F32)
    q_pos = jnp.where(q_live, query_line[0:1] * 256.0 + query_line[1:2], float(pack - 1))
    q_doc = jnp.where(q_live, query_line[2:3], last_doc)
    line8 = lax.broadcasted_iota(jnp.int32, (8, rows), 0)
    q_first = q_doc * 1024.0
    q_ref[...] = jnp.where(line8 == 0, q_first, q_first + q_pos)
    k_row = lax.broadcasted_iota(jnp.int32, (rows, 1), 0).astype(F32)
    for part, (pick, count) in enumerate(((own_pick, own_count), (other_pick, other_count))):
        cols = lax.dot_general(pick, fields, NT, preferred_element_type=F32)
        code = cols[:, 2:3] * 1024.0 + cols[:, 0:1] * 256.0 + cols[:, 1:2]
        code = jnp.where(k_row < count, code, FAR)
        k_ref[part * rows : (part + 1) * rows, :] = jnp.broadcast_to(code, (rows, 128))


def slab_body(at_ref, weight_ref, slab_ref, buf_ref, sems):
    parts, half, wide = slab_ref.shape
    mine = pl.ds(pl.multiple_of(at_ref[2] * half, half), half)
    loads, saves = [], []
    for i in range(parts):
        source = weight_ref.at[at_ref[0], mine, pl.ds(i * wide, wide)]
        loads.append(pltpu.make_async_copy(source, buf_ref.at[i], sems.at[0, i]))
        saves.append(pltpu.make_async_copy(buf_ref.at[i], slab_ref.at[i], sems.at[1, i]))
    for load in loads:
        load.start()
    for load, save in zip(loads, saves):
        load.wait()
        save.start()
    for save in saves:
        save.wait()


def weight_slabs(at, out_weight, parts):
    _, cols, width = out_weight.shape
    shape = (parts, cols // 2, width // parts)
    return pl.pallas_call(
        slab_body,
        out_shape=jax.ShapeDtypeStruct(shape, BF),
        in_specs=[SMEM, HBM],
        out_specs=HBM,
        scratch_shapes=[pltpu.VMEM(shape, BF), pltpu.SemaphoreType.DMA((2, parts))],
        compiler_params=pltpu.CompilerParams(vmem_limit_bytes=60 * 1024 * 1024),
        cost_estimate=cost(0, 2 * cols * width),
        name="weight_slabs",
    )(at, out_weight)


GRAD_STEPS = 8


def prepare_body(
    at_ref, modal_ref, doc_ref, weight_ref, grad_ref, q_ref, k_ref, out_ref, w_buf, g_buf, sems
):
    wide = w_buf.shape[1] // GRAD_STEPS
    copies = []
    for i in range(GRAD_STEPS):
        c = pl.ds(i * wide, wide)
        for n, (src, dst) in enumerate(
            ((weight_ref.at[at_ref[0], :, c], w_buf), (grad_ref.at[:, c], g_buf))
        ):
            copy = pltpu.make_async_copy(src, dst.at[:, c], sems.at[n, i])
            copy.start()
            copies.append(copy)
    codes_into(at_ref[0], modal_ref, doc_ref, q_ref, k_ref)
    total = jnp.zeros(out_ref.shape, F32)
    for i in range(GRAD_STEPS):
        copies[2 * i].wait()
        copies[2 * i + 1].wait()
        c = slice(i * wide, (i + 1) * wide)
        total = total + lax.dot_general(
            g_buf[:, c], w_buf[:, c], NT, preferred_element_type=F32
        )
    out_ref[...] = total.astype(BF)


def prepare(at, modality, doc_ids, out_weight, out_grad):
    _, cols, width = out_weight.shape
    rows = out_grad.shape[0]
    return pl.pallas_call(
        prepare_body,
        out_shape=(
            jax.ShapeDtypeStruct((8, rows), F32),
            jax.ShapeDtypeStruct((2 * rows, 128), F32),
            jax.ShapeDtypeStruct((rows, cols), BF),
        ),
        in_specs=[SMEM, VMEM, VMEM, HBM, HBM],
        out_specs=(VMEM,) * 3,
        scratch_shapes=[
            pltpu.VMEM((cols, width), BF),
            pltpu.VMEM((rows, width), BF),
            pltpu.SemaphoreType.DMA((2, GRAD_STEPS)),
        ],
        compiler_params=pltpu.CompilerParams(vmem_limit_bytes=50 * 1024 * 1024),
        cost_estimate=cost(2 * rows * cols * width, 2 * (cols + rows) * width),
        name="prepare",
    )(at, modality, doc_ids, out_weight, out_grad)


def scores(keys, q, key_code, query_code):
    s = lax.dot_general(keys, q, NT, preferred_element_type=F32) * (HD**-0.5)
    wide = jnp.concatenate([key_code] * (q.shape[0] // 128), axis=1)
    ok = (wide >= query_code[0:1]) & (wide <= query_code[1:2])
    return jnp.where(ok, s, MASKED)


TILE = 256


def attention_body(
    q_ref,
    k_ref,
    v_ref,
    kp_ref,
    vp_ref,
    ga_ref,
    qc_ref,
    kc_ref,
    spread_ref,
    dq_ref,
    own_ref,
    cross_ref,
    w_buf,
    inv_buf,
    att_buf,
    dq_buf,
    own_buf,
    cross_buf,
    sems,
):
    rows, cols = q_ref.shape
    heads = cols // HD
    factor = HD ** (-0.5)
    key_code = kc_ref[...]
    lanes = [slice(h * HD, (h + 1) * HD) for h in range(heads)]
    keys = [jnp.concatenate((k_ref[:, c], kp_ref[:, c])) for c in lanes]
    values = [jnp.concatenate((v_ref[:, c], vp_ref[:, c])) for c in lanes]
    saves = []

    def save(src, dst):
        copy = pltpu.make_async_copy(src, dst, sems.at[len(saves)])
        copy.start()
        saves.append(copy)

    for h, c in enumerate(lanes):
        for t in range(0, rows, TILE):
            r = slice(t, t + TILE)
            s = scores(keys[h], q_ref[r, c], key_code, qc_ref[:, r])
            top = jnp.max(s, axis=0, keepdims=True)
            w = jnp.exp(s - top)
            w_buf[h, :, r] = w
            inv = 1.0 / jnp.sum(w, axis=0, keepdims=True)
            inv_buf[h, :, r] = jnp.broadcast_to(inv, (8, TILE))
            mixed = lax.dot_general(values[h], w.astype(BF), TN, preferred_element_type=F32)
            att_buf[r, c] = jnp.transpose(mixed * inv).astype(BF)
        for x in range(spread_ref.shape[0]):
            save(att_buf.at[:, c], spread_ref.at[x, :, c])
    for h, c in enumerate(lanes):
        dk = jnp.zeros((2 * rows, HD), F32)
        dv = jnp.zeros((2 * rows, HD), F32)
        for t in range(0, rows, TILE):
            r = slice(t, t + TILE)
            ga = ga_ref[r, c]
            both = ga.astype(F32) * att_buf[r, c].astype(F32)
            delta = jnp.sum(jnp.transpose(both), axis=0, keepdims=True)
            prob = w_buf[h, :, r] * inv_buf[h, 0:1, r]
            dp = lax.dot_general(values[h], ga, NT, preferred_element_type=F32)
            ds = (prob * (dp - delta)).astype(BF)
            dq = lax.dot_general(keys[h], ds, TN, preferred_element_type=F32)
            dq_buf[r, c] = jnp.transpose(dq * factor).astype(BF)
            dk = dk + jnp.dot(ds, q_ref[r, c], preferred_element_type=F32)
            dv = dv + jnp.dot(prob.astype(BF), ga, preferred_element_type=F32)
        dk = dk * factor
        for n, grad in enumerate((dk, dv)):
            own_buf[n, :, c] = grad[:rows].astype(BF)
            cross_buf[n, :, c] = grad[rows:].astype(BF)
        save(cross_buf.at[:, :, c], cross_ref.at[:, :, c])
        save(dq_buf.at[:, c], dq_ref.at[:, c])
        save(own_buf.at[:, :, c], own_ref.at[:, :, c])
    for copy in saves:
        copy.wait()


def attention(q, k, v, k_peer, v_peer, ga, codes, copies):
    rows, cols = q.shape
    heads = cols // HD
    outs = (
        jax.ShapeDtypeStruct((copies, rows, cols), BF),
        jax.ShapeDtypeStruct((rows, cols), BF),
        jax.ShapeDtypeStruct((2, rows, cols), BF),
        jax.ShapeDtypeStruct((2, rows, cols), BF),
    )
    return pl.pallas_call(
        attention_body,
        out_shape=outs,
        in_specs=[VMEM] * 8,
        out_specs=(HBM,) * 4,
        scratch_shapes=[
            pltpu.VMEM((heads, 2 * rows, rows), F32),
            pltpu.VMEM((heads, 8, rows), F32),
            pltpu.VMEM((rows, cols), BF),
            pltpu.VMEM((rows, cols), BF),
            pltpu.VMEM((2, rows, cols), BF),
            pltpu.VMEM((2, rows, cols), BF),
            pltpu.SemaphoreType.DMA((heads * (copies + 3),)),
        ],
        compiler_params=pltpu.CompilerParams(vmem_limit_bytes=28 * 1024 * 1024),
        cost_estimate=cost(
            24 * heads * rows * rows * HD, 12 * rows * rows * heads, 2 * heads * rows * rows
        ),
        name="attention",
    )(q, k, v, k_peer, v_peer, ga, *codes)


def project_body(at_ref, att_ref, mine_ref, other_ref, up_ref, down_ref, near_ref, own_ref):
    parts, rows, cols = att_ref.shape
    half = cols // 2
    low, high = slice(0, rows // 2), slice(rows // 2, rows)
    lhs = []
    for which in (at_ref[2], 1 - at_ref[2]):
        lanes = pl.ds(pl.multiple_of(which * half, half), half)
        lhs.append(jnp.concatenate([att_ref[x, :, lanes] for x in range(parts)], axis=1))
    for step in range(4):
        c = pl.ds(pl.multiple_of(((at_ref[3] + step) % 4) * cols, cols), cols)
        total = jnp.zeros((rows, cols), F32)
        for left, right in zip(lhs, (mine_ref, other_ref)):
            right = jnp.concatenate([right[x, :, c] for x in range(parts)], axis=0)
            total = total + jnp.dot(left, right, preferred_element_type=F32)
        total = total.astype(BF)
        if step == 0:
            own_ref[...] = total
        elif step == 1:
            near_ref[0] = total[low]
            up_ref[1] = total[high]
        elif step == 2:
            up_ref[0] = total[low]
            down_ref[0] = total[high]
        else:
            down_ref[1] = total[low]
            near_ref[1] = total[high]


def project(at, att, mine, other):
    parts, rows, cols = att.shape
    halves = jax.ShapeDtypeStruct((2, rows // 2, cols), BF)
    return pl.pallas_call(
        project_body,
        out_shape=(halves, halves, halves, jax.ShapeDtypeStruct((rows, cols), BF)),
        in_specs=[SMEM] + [VMEM] * 3,
        out_specs=(VMEM,) * 4,
        compiler_params=pltpu.CompilerParams(vmem_limit_bytes=12 * 1024 * 1024),
        cost_estimate=cost(8 * parts * rows * cols * cols, 4 * mine.size + 4 * att.size),
        name="project",
    )(at, att, mine, other)


def ring_sum(up, down, near, own):
    size = lax.axis_size("y")
    rise = [(i, (i + 1) % size) for i in range(size)]
    fall = [(i, (i - 1) % size) for i in range(size)]
    from_below = lax.ppermute(up, "y", rise)
    from_above = lax.ppermute(down, "y", fall)
    next_up = (near[0].astype(F32) + from_below[0].astype(F32)).astype(BF)
    next_down = (near[1].astype(F32) + from_above[0].astype(F32)).astype(BF)
    low = lax.ppermute(next_up, "y", rise)
    high = lax.ppermute(next_down, "y", fall)
    others = jnp.concatenate(
        (from_above[1].astype(F32) + low.astype(F32), from_below[1].astype(F32) + high.astype(F32))
    )
    return (own.astype(F32) + others).astype(BF)


def finish_body(own_ref, back_ref, dk_ref, dv_ref):
    dk_ref[...] = (own_ref[0].astype(F32) + back_ref[0].astype(F32)).astype(BF)
    dv_ref[...] = (own_ref[1].astype(F32) + back_ref[1].astype(F32)).astype(BF)


def finish(own, back):
    shape = jax.ShapeDtypeStruct(own.shape[1:], BF)
    return pl.pallas_call(
        finish_body,
        out_shape=(shape, shape),
        in_specs=[VMEM] * 2,
        out_specs=(VMEM,) * 2,
        compiler_params=pltpu.CompilerParams(vmem_limit_bytes=60 * 1024 * 1024),
        cost_estimate=cost(own.size, 8 * own.size),
        name="finish",
    )(own, back)


def step(query_heads, key_heads, value_heads, modality, doc_ids, out_weight, out_grad):
    at = jnp.stack([lax.axis_index(a).astype(jnp.int32) for a in ("side", "x", "core", "y")])
    swap = [(0, 1), (1, 0)]
    xs = lax.axis_size("x")
    k_peer = lax.ppermute(key_heads, "side", swap)
    v_peer = lax.ppermute(value_heads, "side", swap)
    slabs = weight_slabs(at, out_weight, xs)
    mine = lax.all_to_all(slabs, "x", 0, 0, tiled=True)
    modality, _ = lax.optimization_barrier((modality, slabs))
    query_code, key_code, grad_attended = prepare(
        at, modality, doc_ids, out_weight, out_grad
    )
    spread, grad_query, own, cross = attention(
        query_heads,
        key_heads,
        value_heads,
        k_peer,
        v_peer,
        grad_attended,
        (query_code, key_code),
        xs,
    )
    gathered = lax.all_to_all(spread, "x", 0, 0, tiled=True)
    other = lax.ppermute(mine, "core", swap)
    returned = lax.ppermute(cross, "side", swap)
    pieces = project(at, gathered, mine, other)
    layer_output = ring_sum(*pieces)
    grad_key, grad_value = finish(own, returned)
    return (layer_output, grad_query, grad_key, grad_value)


def solution(mesh):
    groups, _ = mesh.devices.shape
    split = Mesh(mesh.devices.reshape(2, groups // 4, 2, 4, 4), ("side", "z", "core", "x", "y"))
    grp, tp = ("side", "z", "core"), ("x", "y")
    tokens = P(grp, tp)
    placed = (
        tokens,
        tokens,
        tokens,
        P(grp, None),
        P(grp, None),
        P(None, tp, None),
        P(grp, None),
    )
    return jax.shard_map(
        step,
        mesh=split,
        in_specs=placed,
        out_specs=(tokens, tokens, tokens, tokens),
        check_vma=False,
    )
```

```python
import jax
import jax.numpy as jnp
from jax import lax
from jax.experimental import pallas as pl
from jax.experimental.pallas import tpu as pltpu
from jax.sharding import Mesh, PartitionSpec as P

HD = 128
MASKED = -1e30
FAR = 1e6
BF = jnp.bfloat16
F32 = jnp.float32
VMEM = pl.BlockSpec(memory_space=pltpu.VMEM)
SMEM = pl.BlockSpec(memory_space=pltpu.SMEM)
HBM = pl.BlockSpec(memory_space=pltpu.HBM)
NT = (((1,), (1,)), ((), ()))
TN = (((0,), (0,)), ((), ()))


def cost(flops, nbytes, exps=0):
    return pl.CostEstimate(flops=flops, bytes_accessed=nbytes, transcendentals=exps)


def codes_into(side, modal_ref, doc_ref, q_ref, k_ref):
    pack = modal_ref.shape[1]
    rows = q_ref.shape[1]
    own = (modal_ref[...] == side).astype(F32)
    other = 1.0 - own
    row8 = lax.broadcasted_iota(jnp.int32, (8, pack), 0)
    both = jnp.where(row8 == 0, own, other).astype(BF)
    before = lax.broadcasted_iota(jnp.int32, (pack, pack), 0) <= lax.broadcasted_iota(
        jnp.int32, (pack, pack), 1
    )
    upto = jnp.where(before, 1.0, 0.0).astype(BF)
    ranks = jnp.dot(both, upto, preferred_element_type=F32)
    slot = lax.broadcasted_iota(jnp.int32, (rows, pack), 0).astype(F32)
    spot = lax.broadcasted_iota(jnp.int32, (128, pack), 1)
    line = lax.broadcasted_iota(jnp.int32, (128, pack), 0)
    docs = doc_ref[...]
    fields = jnp.where(
        line == 0, spot // 256, jnp.where(line == 1, spot % 256, jnp.where(line == 2, docs, 0))
    )
    fields = fields.astype(F32).astype(BF)

    def picked(chosen, rank):
        code = jnp.where(chosen > 0.5, rank - 1.0, -1.0)
        return jnp.where(slot == code, 1.0, 0.0).astype(BF)

    own_pick = picked(own, ranks[0:1])
    other_pick = picked(other, ranks[1:2])
    own_count = ranks[0:1, pack - 1 : pack]
    other_count = ranks[1:2, pack - 1 : pack]
    query_line = lax.dot_general(fields, own_pick, NT, preferred_element_type=F32)
    q_live = lax.broadcasted_iota(jnp.int32, (1, rows), 1).astype(F32) < own_count
    last_doc = docs[0:1, pack - 1 : pack].astype(F32)
    q_pos = jnp.where(q_live, query_line[0:1] * 256.0 + query_line[1:2], float(pack - 1))
    q_doc = jnp.where(q_live, query_line[2:3], last_doc)
    line8 = lax.broadcasted_iota(jnp.int32, (8, rows), 0)
    q_first = q_doc * 1024.0
    q_ref[...] = jnp.where(line8 == 0, q_first, q_first + q_pos)
    k_row = lax.broadcasted_iota(jnp.int32, (rows, 1), 0).astype(F32)
    for part, (pick, count) in enumerate(((own_pick, own_count), (other_pick, other_count))):
        cols = lax.dot_general(pick, fields, NT, preferred_element_type=F32)
        code = cols[:, 2:3] * 1024.0 + cols[:, 0:1] * 256.0 + cols[:, 1:2]
        code = jnp.where(k_row < count, code, FAR)
        k_ref[part * rows : (part + 1) * rows, :] = jnp.broadcast_to(code, (rows, 128))


GRAD_STEPS = 8


def prepare_body(
    at_ref, modal_ref, doc_ref, weight_ref, grad_ref, q_ref, k_ref, out_ref, w_buf, g_buf, sems
):
    wide = w_buf.shape[1] // GRAD_STEPS
    copies = []
    for i in range(GRAD_STEPS):
        c = pl.ds(i * wide, wide)
        for n, (src, dst) in enumerate(
            ((weight_ref.at[at_ref[0], :, c], w_buf), (grad_ref.at[:, c], g_buf))
        ):
            copy = pltpu.make_async_copy(src, dst.at[:, c], sems.at[n, i])
            copy.start()
            copies.append(copy)
    codes_into(at_ref[0], modal_ref, doc_ref, q_ref, k_ref)
    total = jnp.zeros(out_ref.shape, F32)
    for i in range(GRAD_STEPS):
        copies[2 * i].wait()
        copies[2 * i + 1].wait()
        c = slice(i * wide, (i + 1) * wide)
        total = total + lax.dot_general(
            g_buf[:, c], w_buf[:, c], NT, preferred_element_type=F32
        )
    out_ref[...] = total.astype(BF)


def prepare(at, modality, doc_ids, out_weight, out_grad):
    _, cols, width = out_weight.shape
    rows = out_grad.shape[0]
    return pl.pallas_call(
        prepare_body,
        out_shape=(
            jax.ShapeDtypeStruct((8, rows), F32),
            jax.ShapeDtypeStruct((2 * rows, 128), F32),
            jax.ShapeDtypeStruct((rows, cols), BF),
        ),
        in_specs=[SMEM, VMEM, VMEM, HBM, HBM],
        out_specs=(VMEM,) * 3,
        scratch_shapes=[
            pltpu.VMEM((cols, width), BF),
            pltpu.VMEM((rows, width), BF),
            pltpu.SemaphoreType.DMA((2, GRAD_STEPS)),
        ],
        compiler_params=pltpu.CompilerParams(vmem_limit_bytes=50 * 1024 * 1024),
        cost_estimate=cost(2 * rows * cols * width, 2 * (cols + rows) * width),
        name="prepare",
    )(at, modality, doc_ids, out_weight, out_grad)


def scores(keys, q, key_code, query_code):
    s = lax.dot_general(keys, q, NT, preferred_element_type=F32) * (HD**-0.5)
    wide = jnp.concatenate([key_code] * (q.shape[0] // 128), axis=1)
    ok = (wide >= query_code[0:1]) & (wide <= query_code[1:2])
    return jnp.where(ok, s, MASKED)


TILE = 256


def attention_body(
    q_ref,
    k_ref,
    v_ref,
    peer_ref,
    ga_ref,
    qc_ref,
    kc_ref,
    spread_ref,
    dq_ref,
    own_ref,
    cross_ref,
    w_buf,
    inv_buf,
    att_buf,
    dq_buf,
    own_buf,
    cross_buf,
    sems,
):
    rows, cols = q_ref.shape
    heads = cols // HD
    factor = HD ** (-0.5)
    key_code = kc_ref[...]
    lanes = [slice(h * HD, (h + 1) * HD) for h in range(heads)]
    keys = [jnp.concatenate((k_ref[:, c], peer_ref[0, :, c])) for c in lanes]
    values = [jnp.concatenate((v_ref[:, c], peer_ref[1, :, c])) for c in lanes]
    saves = []

    def save(src, dst):
        copy = pltpu.make_async_copy(src, dst, sems.at[len(saves)])
        copy.start()
        saves.append(copy)

    for h, c in enumerate(lanes):
        for t in range(0, rows, TILE):
            r = slice(t, t + TILE)
            s = scores(keys[h], q_ref[r, c], key_code, qc_ref[:, r])
            top = jnp.max(s, axis=0, keepdims=True)
            w = jnp.exp(s - top)
            w_buf[h, :, r] = w
            inv = 1.0 / jnp.sum(w, axis=0, keepdims=True)
            inv_buf[h, :, r] = jnp.broadcast_to(inv, (8, TILE))
            mixed = lax.dot_general(values[h], w.astype(BF), TN, preferred_element_type=F32)
            att_buf[r, c] = jnp.transpose(mixed * inv).astype(BF)
        for x in range(spread_ref.shape[0]):
            save(att_buf.at[:, c], spread_ref.at[x, :, c])
    for h, c in enumerate(lanes):
        dk = jnp.zeros((2 * rows, HD), F32)
        dv = jnp.zeros((2 * rows, HD), F32)
        for t in range(0, rows, TILE):
            r = slice(t, t + TILE)
            ga = ga_ref[r, c]
            both = ga.astype(F32) * att_buf[r, c].astype(F32)
            delta = jnp.sum(jnp.transpose(both), axis=0, keepdims=True)
            prob = w_buf[h, :, r] * inv_buf[h, 0:1, r]
            dp = lax.dot_general(values[h], ga, NT, preferred_element_type=F32)
            ds = (prob * (dp - delta)).astype(BF)
            dq = lax.dot_general(keys[h], ds, TN, preferred_element_type=F32)
            dq_buf[r, c] = jnp.transpose(dq * factor).astype(BF)
            dk = dk + jnp.dot(ds, q_ref[r, c], preferred_element_type=F32)
            dv = dv + jnp.dot(prob.astype(BF), ga, preferred_element_type=F32)
        dk = dk * factor
        for n, grad in enumerate((dk, dv)):
            own_buf[n, :, c] = grad[:rows].astype(BF)
            cross_buf[n, :, c] = grad[rows:].astype(BF)
        save(cross_buf.at[:, :, c], cross_ref.at[:, :, c])
        save(dq_buf.at[:, c], dq_ref.at[:, c])
        save(own_buf.at[:, :, c], own_ref.at[:, :, c])
    for copy in saves:
        copy.wait()


def attention(q, k, v, peer, ga, codes, copies):
    rows, cols = q.shape
    heads = cols // HD
    outs = (
        jax.ShapeDtypeStruct((copies, rows, cols), BF),
        jax.ShapeDtypeStruct((rows, cols), BF),
        jax.ShapeDtypeStruct((2, rows, cols), BF),
        jax.ShapeDtypeStruct((2, rows, cols), BF),
    )
    return pl.pallas_call(
        attention_body,
        out_shape=outs,
        in_specs=[VMEM] * 7,
        out_specs=(HBM,) * 4,
        scratch_shapes=[
            pltpu.VMEM((heads, 2 * rows, rows), F32),
            pltpu.VMEM((heads, 8, rows), F32),
            pltpu.VMEM((rows, cols), BF),
            pltpu.VMEM((rows, cols), BF),
            pltpu.VMEM((2, rows, cols), BF),
            pltpu.VMEM((2, rows, cols), BF),
            pltpu.SemaphoreType.DMA((heads * (copies + 3),)),
        ],
        compiler_params=pltpu.CompilerParams(vmem_limit_bytes=28 * 1024 * 1024),
        cost_estimate=cost(
            24 * heads * rows * rows * HD, 12 * rows * rows * heads, 2 * heads * rows * rows
        ),
        name="attention",
    )(q, k, v, peer, ga, *codes)


def project_body(at_ref, att_ref, mine_ref, other_ref, out_ref):
    parts, rows, cols = att_ref.shape
    half = cols // 2
    lhs = []
    for which in (at_ref[2], 1 - at_ref[2]):
        lanes = pl.ds(pl.multiple_of(which * half, half), half)
        lhs.append(jnp.concatenate([att_ref[x, :, lanes] for x in range(parts)], axis=1))
    for n in range(out_ref.shape[0]):
        c = slice(n * cols, (n + 1) * cols)
        total = jnp.zeros((rows, cols), F32)
        for left, right in zip(lhs, (mine_ref, other_ref)):
            right = jnp.concatenate([right[x, :, c] for x in range(parts)], axis=0)
            total = total + jnp.dot(left, right, preferred_element_type=F32)
        out_ref[n] = total.astype(BF)


def project(at, att, mine, other):
    parts, rows, cols = att.shape
    outs = mine.shape[2] // cols
    return pl.pallas_call(
        project_body,
        out_shape=jax.ShapeDtypeStruct((outs, rows, cols), BF),
        in_specs=[SMEM] + [VMEM] * 3,
        out_specs=VMEM,
        compiler_params=pltpu.CompilerParams(vmem_limit_bytes=12 * 1024 * 1024),
        cost_estimate=cost(2 * parts * rows * cols * outs * cols, 4 * mine.size + 4 * att.size),
        name="project",
    )(at, att, mine, other)


def finish_body(own_ref, back_ref, dk_ref, dv_ref):
    dk_ref[...] = (own_ref[0].astype(F32) + back_ref[0].astype(F32)).astype(BF)
    dv_ref[...] = (own_ref[1].astype(F32) + back_ref[1].astype(F32)).astype(BF)


def finish(own, back):
    shape = jax.ShapeDtypeStruct(own.shape[1:], BF)
    return pl.pallas_call(
        finish_body,
        out_shape=(shape, shape),
        in_specs=[VMEM] * 2,
        out_specs=(VMEM,) * 2,
        compiler_params=pltpu.CompilerParams(vmem_limit_bytes=60 * 1024 * 1024),
        cost_estimate=cost(own.size, 8 * own.size),
        name="finish",
    )(own, back)


def step(query_heads, key_heads, value_heads, modality, doc_ids, out_weight, out_grad):
    _, cols = query_heads.shape
    at = jnp.stack([lax.axis_index(a).astype(jnp.int32) for a in ("side", "x", "core")])
    swap = [(0, 1), (1, 0)]
    xs = lax.axis_size("x")
    peer = lax.ppermute(jnp.stack((key_heads, value_heads)), "side", swap)
    half, wide = cols // 2, out_weight.shape[2] // xs
    side, core = lax.axis_index("side"), lax.axis_index("core")
    slabs = jnp.concatenate(
        [
            lax.dynamic_slice(out_weight, (side, core * half, i * wide), (1, half, wide))
            for i in range(xs)
        ]
    )
    mine = lax.all_to_all(slabs, "x", 0, 0, tiled=True)
    modality, _ = lax.optimization_barrier((modality, slabs))
    query_code, key_code, grad_attended = prepare(
        at, modality, doc_ids, out_weight, out_grad
    )
    spread, grad_query, own, cross = attention(
        query_heads,
        key_heads,
        value_heads,
        peer,
        grad_attended,
        (query_code, key_code),
        xs,
    )
    gathered = lax.all_to_all(spread, "x", 0, 0, tiled=True)
    other = lax.ppermute(mine, "core", swap)
    returned = lax.ppermute(cross, "side", swap)
    partial = project(at, gathered, mine, other)
    pieces = lax.all_to_all(partial, "y", 0, 0, tiled=True)
    layer_output = jnp.sum(pieces.astype(F32), axis=0).astype(BF)
    grad_key, grad_value = finish(own, returned)
    return (layer_output, grad_query, grad_key, grad_value)


def solution(mesh):
    groups, _ = mesh.devices.shape
    split = Mesh(mesh.devices.reshape(2, groups // 4, 2, 4, 4), ("side", "z", "core", "x", "y"))
    grp, tp = ("side", "z", "core"), ("x", "y")
    tokens = P(grp, tp)
    placed = (
        tokens,
        tokens,
        tokens,
        P(grp, None),
        P(grp, None),
        P(None, tp, None),
        P(grp, None),
    )
    return jax.shard_map(
        step,
        mesh=split,
        in_specs=placed,
        out_specs=(tokens, tokens, tokens, tokens),
        check_vma=False,
    )
```

```python
import jax
import jax.numpy as jnp
from jax import lax
from jax.experimental import pallas as pl
from jax.experimental.pallas import tpu as pltpu
from jax.sharding import Mesh, PartitionSpec as P

HD = 128
MASKED = -1e30
LOG2E = 1.4426950408889634
FAR = 1e6
BF = jnp.bfloat16
F32 = jnp.float32
VMEM = pl.BlockSpec(memory_space=pltpu.VMEM)
SMEM = pl.BlockSpec(memory_space=pltpu.SMEM)
HBM = pl.BlockSpec(memory_space=pltpu.HBM)
NT = (((1,), (1,)), ((), ()))
TN = (((0,), (0,)), ((), ()))


def cost(flops, nbytes, exps=0):
    return pl.CostEstimate(flops=flops, bytes_accessed=nbytes, transcendentals=exps)


def codes_into(side, modal_ref, doc_ref, q_ref, k_ref):
    pack = modal_ref.shape[1]
    rows = q_ref.shape[1]
    own = (modal_ref[...] == side).astype(F32)
    other = 1.0 - own
    row8 = lax.broadcasted_iota(jnp.int32, (8, pack), 0)
    both = jnp.where(row8 == 0, own, other).astype(BF)
    before = lax.broadcasted_iota(jnp.int32, (pack, pack), 0) <= lax.broadcasted_iota(
        jnp.int32, (pack, pack), 1
    )
    upto = jnp.where(before, 1.0, 0.0).astype(BF)
    ranks = jnp.dot(both, upto, preferred_element_type=F32)
    slot = lax.broadcasted_iota(jnp.int32, (rows, pack), 0).astype(F32)
    spot = lax.broadcasted_iota(jnp.int32, (128, pack), 1)
    line = lax.broadcasted_iota(jnp.int32, (128, pack), 0)
    docs = doc_ref[...]
    fields = jnp.where(
        line == 0, spot // 256, jnp.where(line == 1, spot % 256, jnp.where(line == 2, docs, 0))
    )
    fields = fields.astype(F32).astype(BF)

    def picked(chosen, rank):
        code = jnp.where(chosen > 0.5, rank - 1.0, -1.0)
        return jnp.where(slot == code, 1.0, 0.0).astype(BF)

    own_pick = picked(own, ranks[0:1])
    other_pick = picked(other, ranks[1:2])
    own_count = ranks[0:1, pack - 1 : pack]
    other_count = ranks[1:2, pack - 1 : pack]
    query_line = lax.dot_general(fields, own_pick, NT, preferred_element_type=F32)
    q_live = lax.broadcasted_iota(jnp.int32, (1, rows), 1).astype(F32) < own_count
    last_doc = docs[0:1, pack - 1 : pack].astype(F32)
    q_pos = jnp.where(q_live, query_line[0:1] * 256.0 + query_line[1:2], float(pack - 1))
    q_doc = jnp.where(q_live, query_line[2:3], last_doc)
    line8 = lax.broadcasted_iota(jnp.int32, (8, rows), 0)
    q_first = q_doc * 1024.0
    q_ref[...] = jnp.where(line8 == 0, q_first, q_first + q_pos)
    k_row = lax.broadcasted_iota(jnp.int32, (rows, 1), 0).astype(F32)
    for part, (pick, count) in enumerate(((own_pick, own_count), (other_pick, other_count))):
        cols = lax.dot_general(pick, fields, NT, preferred_element_type=F32)
        code = cols[:, 2:3] * 1024.0 + cols[:, 0:1] * 256.0 + cols[:, 1:2]
        code = jnp.where(k_row < count, code, FAR)
        k_ref[part * rows : (part + 1) * rows, :] = jnp.broadcast_to(code, (rows, 128))


GRAD_STEPS = 8


def prepare_body(
    at_ref, modal_ref, doc_ref, weight_ref, grad_ref, q_ref, k_ref, out_ref, w_buf, g_buf, sems
):
    wide = w_buf.shape[1] // GRAD_STEPS
    copies = []
    for i in range(GRAD_STEPS):
        c = pl.ds(i * wide, wide)
        for n, (src, dst) in enumerate(
            ((weight_ref.at[at_ref[0], :, c], w_buf), (grad_ref.at[:, c], g_buf))
        ):
            copy = pltpu.make_async_copy(src, dst.at[:, c], sems.at[n, i])
            copy.start()
            copies.append(copy)
    codes_into(at_ref[0], modal_ref, doc_ref, q_ref, k_ref)
    total = jnp.zeros(out_ref.shape, F32)
    for i in range(GRAD_STEPS):
        copies[2 * i].wait()
        copies[2 * i + 1].wait()
        c = slice(i * wide, (i + 1) * wide)
        total = total + lax.dot_general(
            g_buf[:, c], w_buf[:, c], NT, preferred_element_type=F32
        )
    out_ref[...] = total.astype(BF)


def prepare(at, modality, doc_ids, out_weight, out_grad):
    _, cols, width = out_weight.shape
    rows = out_grad.shape[0]
    return pl.pallas_call(
        prepare_body,
        out_shape=(
            jax.ShapeDtypeStruct((8, rows), F32),
            jax.ShapeDtypeStruct((2 * rows, 128), F32),
            jax.ShapeDtypeStruct((rows, cols), BF),
        ),
        in_specs=[SMEM, VMEM, VMEM, HBM, HBM],
        out_specs=(VMEM,) * 3,
        scratch_shapes=[
            pltpu.VMEM((cols, width), BF),
            pltpu.VMEM((rows, width), BF),
            pltpu.SemaphoreType.DMA((2, GRAD_STEPS)),
        ],
        compiler_params=pltpu.CompilerParams(vmem_limit_bytes=50 * 1024 * 1024),
        cost_estimate=cost(2 * rows * cols * width, 2 * (cols + rows) * width),
        name="prepare",
    )(at, modality, doc_ids, out_weight, out_grad)


TILE = 256


def attention_body(
    q_ref,
    k_ref,
    v_ref,
    peer_ref,
    ga_ref,
    qc_ref,
    kc_ref,
    spread_ref,
    dq_ref,
    own_ref,
    cross_ref,
    w_buf,
    inv_buf,
    att_buf,
    dq_buf,
    own_buf,
    cross_buf,
    sems,
):
    rows, cols = q_ref.shape
    heads = cols // HD
    factor = HD ** (-0.5)
    scale = factor * LOG2E
    lanes = [slice(h * HD, (h + 1) * HD) for h in range(heads)]

    saves = []

    def save(src, dst):
        copy = pltpu.make_async_copy(src, dst, sems.at[len(saves)])
        copy.start()
        saves.append(copy)

    for t in range(0, rows, TILE):
        r = slice(t, t + TILE)
        seen = t + TILE
        code = jnp.concatenate((kc_ref[:seen], kc_ref[rows:]))
        code = jnp.concatenate([code] * (TILE // 128), axis=1)
        ok = (code >= qc_ref[0:1, r]) & (code <= qc_ref[1:2, r])
        bias = jnp.where(ok, 0.0, MASKED)
        for h, c in enumerate(lanes):
            keys = jnp.concatenate((k_ref[:seen, c], peer_ref[0, :, c]))
            values = jnp.concatenate((v_ref[:seen, c], peer_ref[1, :, c]))
            s = lax.dot_general(keys, q_ref[r, c], NT, preferred_element_type=F32)
            s = s * scale + bias
            w = jnp.exp2(s - jnp.max(s, axis=0, keepdims=True))
            w_buf[h, : seen + rows, r] = w
            inv = 1.0 / jnp.sum(w, axis=0, keepdims=True)
            inv_buf[h, :, r] = jnp.broadcast_to(inv, (8, TILE))
            mixed = lax.dot_general(values, w.astype(BF), TN, preferred_element_type=F32)
            att_buf[r, c] = jnp.transpose(mixed * inv).astype(BF)
    for x in range(spread_ref.shape[0]):
        save(att_buf, spread_ref.at[x])
    for h, c in enumerate(lanes):
        sums = []
        for t in range(0, rows, TILE):
            r = slice(t, t + TILE)
            seen = t + TILE
            keys = jnp.concatenate((k_ref[:seen, c], peer_ref[0, :, c]))
            values = jnp.concatenate((v_ref[:seen, c], peer_ref[1, :, c]))
            ga = ga_ref[r, c]
            both = ga.astype(F32) * att_buf[r, c].astype(F32)
            delta = jnp.sum(jnp.transpose(both), axis=0, keepdims=True)
            prob = w_buf[h, : seen + rows, r] * inv_buf[h, 0:1, r]
            dp = lax.dot_general(values, ga, NT, preferred_element_type=F32)
            ds = (prob * (dp - delta)).astype(BF)
            dq = lax.dot_general(keys, ds, TN, preferred_element_type=F32)
            dq_buf[r, c] = jnp.transpose(dq * factor).astype(BF)
            sums.append(
                (
                    jnp.dot(ds, q_ref[r, c], preferred_element_type=F32) * factor,
                    jnp.dot(prob.astype(BF), ga, preferred_element_type=F32),
                )
            )
        dk, dv = [
            jnp.concatenate(
                (one[:TILE] + two[:TILE], two[TILE:rows], one[TILE:] + two[rows:])
            )
            for one, two in zip(*sums)
        ]
        for n, grad in enumerate((dk, dv)):
            own_buf[n, :, c] = grad[:rows].astype(BF)
            cross_buf[n, :, c] = grad[rows:].astype(BF)
        save(cross_buf.at[:, :, c], cross_ref.at[:, :, c])
        save(dq_buf.at[:, c], dq_ref.at[:, c])
        save(own_buf.at[:, :, c], own_ref.at[:, :, c])
    for copy in saves:
        copy.wait()


def attention(q, k, v, peer, ga, codes, copies):
    rows, cols = q.shape
    heads = cols // HD
    outs = (
        jax.ShapeDtypeStruct((copies, rows, cols), BF),
        jax.ShapeDtypeStruct((rows, cols), BF),
        jax.ShapeDtypeStruct((2, rows, cols), BF),
        jax.ShapeDtypeStruct((2, rows, cols), BF),
    )
    return pl.pallas_call(
        attention_body,
        out_shape=outs,
        in_specs=[VMEM] * 7,
        out_specs=(HBM,) * 4,
        scratch_shapes=[
            pltpu.VMEM((heads, 2 * rows, rows), F32),
            pltpu.VMEM((heads, 8, rows), F32),
            pltpu.VMEM((rows, cols), BF),
            pltpu.VMEM((rows, cols), BF),
            pltpu.VMEM((2, rows, cols), BF),
            pltpu.VMEM((2, rows, cols), BF),
            pltpu.SemaphoreType.DMA((heads * 3 + copies,)),
        ],
        compiler_params=pltpu.CompilerParams(vmem_limit_bytes=28 * 1024 * 1024),
        cost_estimate=cost(
            24 * heads * rows * rows * HD, 12 * rows * rows * heads, 2 * heads * rows * rows
        ),
        name="attention",
    )(q, k, v, peer, ga, *codes)


def project_body(at_ref, att_ref, mine_ref, other_ref, out_ref, buf_ref, sems):
    parts, rows, cols = att_ref.shape
    half = cols // 2
    lhs, saves = [], []
    for which in (at_ref[2], 1 - at_ref[2]):
        lanes = pl.ds(pl.multiple_of(which * half, half), half)
        lhs.append(jnp.concatenate([att_ref[x, :, lanes] for x in range(parts)], axis=1))
    for n in range(out_ref.shape[0]):
        c = slice(n * cols, (n + 1) * cols)
        total = jnp.zeros((rows, cols), F32)
        for left, right in zip(lhs, (mine_ref, other_ref)):
            right = jnp.concatenate([right[x, :, c] for x in range(parts)], axis=0)
            total = total + jnp.dot(left, right, preferred_element_type=F32)
        buf_ref[n] = total.astype(BF)
        saves.append(pltpu.make_async_copy(buf_ref.at[n], out_ref.at[n], sems.at[n]))
        saves[-1].start()
    for save in saves:
        save.wait()


def project(at, att, mine, other):
    parts, rows, cols = att.shape
    outs = mine.shape[2] // cols
    return pl.pallas_call(
        project_body,
        out_shape=jax.ShapeDtypeStruct((outs, rows, cols), BF),
        in_specs=[SMEM] + [VMEM] * 3,
        out_specs=HBM,
        scratch_shapes=[pltpu.VMEM((outs, rows, cols), BF), pltpu.SemaphoreType.DMA((outs,))],
        compiler_params=pltpu.CompilerParams(vmem_limit_bytes=12 * 1024 * 1024),
        cost_estimate=cost(2 * parts * rows * cols * outs * cols, 4 * mine.size + 4 * att.size),
        name="project",
    )(at, att, mine, other)


def finish_body(own_ref, back_ref, dk_ref, dv_ref):
    dk_ref[...] = (own_ref[0].astype(F32) + back_ref[0].astype(F32)).astype(BF)
    dv_ref[...] = (own_ref[1].astype(F32) + back_ref[1].astype(F32)).astype(BF)


def finish(own, back):
    shape = jax.ShapeDtypeStruct(own.shape[1:], BF)
    return pl.pallas_call(
        finish_body,
        out_shape=(shape, shape),
        in_specs=[VMEM] * 2,
        out_specs=(VMEM,) * 2,
        compiler_params=pltpu.CompilerParams(vmem_limit_bytes=60 * 1024 * 1024),
        cost_estimate=cost(own.size, 8 * own.size),
        name="finish",
    )(own, back)


def step(query_heads, key_heads, value_heads, modality, doc_ids, out_weight, out_grad):
    _, cols = query_heads.shape
    at = jnp.stack([lax.axis_index(a).astype(jnp.int32) for a in ("side", "x", "core")])
    swap = [(0, 1), (1, 0)]
    xs = lax.axis_size("x")
    peer = lax.ppermute(jnp.stack((key_heads, value_heads)), "side", swap)
    half, wide = cols // 2, out_weight.shape[2] // xs
    side, core = lax.axis_index("side"), lax.axis_index("core")
    slabs = jnp.concatenate(
        [
            lax.dynamic_slice(out_weight, (side, core * half, i * wide), (1, half, wide))
            for i in range(xs)
        ]
    )
    mine = lax.all_to_all(slabs, "x", 0, 0, tiled=True)
    modality, _ = lax.optimization_barrier((modality, slabs))
    query_code, key_code, grad_attended = prepare(
        at, modality, doc_ids, out_weight, out_grad
    )
    spread, grad_query, own, cross = attention(
        query_heads,
        key_heads,
        value_heads,
        peer,
        grad_attended,
        (query_code, key_code),
        xs,
    )
    gathered = lax.all_to_all(spread, "x", 0, 0, tiled=True)
    other = lax.ppermute(mine, "core", swap)
    returned = lax.ppermute(cross, "side", swap)
    partial = project(at, gathered, mine, other)
    pieces = lax.all_to_all(partial, "y", 0, 0, tiled=True)
    layer_output = jnp.sum(pieces.astype(F32), axis=0).astype(BF)
    grad_key, grad_value = finish(own, returned)
    return (layer_output, grad_query, grad_key, grad_value)


def solution(mesh):
    groups, _ = mesh.devices.shape
    split = Mesh(mesh.devices.reshape(2, groups // 4, 2, 4, 4), ("side", "z", "core", "x", "y"))
    grp, tp = ("side", "z", "core"), ("x", "y")
    tokens = P(grp, tp)
    placed = (
        tokens,
        tokens,
        tokens,
        P(grp, None),
        P(grp, None),
        P(None, tp, None),
        P(grp, None),
    )
    return jax.shard_map(
        step,
        mesh=split,
        in_specs=placed,
        out_specs=(tokens, tokens, tokens, tokens),
        check_vma=False,
    )
```

```python
import jax
import jax.numpy as jnp
from jax import lax
from jax.experimental import pallas as pl
from jax.experimental.pallas import tpu as pltpu
from jax.sharding import Mesh, PartitionSpec as P

HD = 128
MASKED = -1e30
LOG2E = 1.4426950408889634
FAR = 1e6
BF = jnp.bfloat16
F32 = jnp.float32
VMEM = pl.BlockSpec(memory_space=pltpu.VMEM)
SMEM = pl.BlockSpec(memory_space=pltpu.SMEM)
HBM = pl.BlockSpec(memory_space=pltpu.HBM)
NT = (((1,), (1,)), ((), ()))
TN = (((0,), (0,)), ((), ()))


def cost(flops, nbytes, exps=0):
    return pl.CostEstimate(flops=flops, bytes_accessed=nbytes, transcendentals=exps)


def codes_into(side, modal_ref, doc_ref, q_ref, k_ref):
    pack = modal_ref.shape[1]
    rows = q_ref.shape[1]
    own = (modal_ref[...] == side).astype(F32)
    other = 1.0 - own
    row8 = lax.broadcasted_iota(jnp.int32, (8, pack), 0)
    both = jnp.where(row8 == 0, own, other).astype(BF)
    before = lax.broadcasted_iota(jnp.int32, (pack, pack), 0) <= lax.broadcasted_iota(
        jnp.int32, (pack, pack), 1
    )
    upto = jnp.where(before, 1.0, 0.0).astype(BF)
    ranks = jnp.dot(both, upto, preferred_element_type=F32)
    slot = lax.broadcasted_iota(jnp.int32, (rows, pack), 0).astype(F32)
    spot = lax.broadcasted_iota(jnp.int32, (128, pack), 1)
    line = lax.broadcasted_iota(jnp.int32, (128, pack), 0)
    docs = doc_ref[...]
    fields = jnp.where(
        line == 0, spot // 256, jnp.where(line == 1, spot % 256, jnp.where(line == 2, docs, 0))
    )
    fields = fields.astype(F32).astype(BF)

    def picked(chosen, rank):
        code = jnp.where(chosen > 0.5, rank - 1.0, -1.0)
        return jnp.where(slot == code, 1.0, 0.0).astype(BF)

    own_pick = picked(own, ranks[0:1])
    other_pick = picked(other, ranks[1:2])
    own_count = ranks[0:1, pack - 1 : pack]
    other_count = ranks[1:2, pack - 1 : pack]
    query_line = lax.dot_general(fields, own_pick, NT, preferred_element_type=F32)
    q_live = lax.broadcasted_iota(jnp.int32, (1, rows), 1).astype(F32) < own_count
    last_doc = docs[0:1, pack - 1 : pack].astype(F32)
    q_pos = jnp.where(q_live, query_line[0:1] * 256.0 + query_line[1:2], float(pack - 1))
    q_doc = jnp.where(q_live, query_line[2:3], last_doc)
    line8 = lax.broadcasted_iota(jnp.int32, (8, rows), 0)
    q_first = q_doc * 1024.0
    q_ref[...] = jnp.where(line8 == 0, q_first, q_first + q_pos)
    k_row = lax.broadcasted_iota(jnp.int32, (rows, 1), 0).astype(F32)
    for part, (pick, count) in enumerate(((own_pick, own_count), (other_pick, other_count))):
        cols = lax.dot_general(pick, fields, NT, preferred_element_type=F32)
        code = cols[:, 2:3] * 1024.0 + cols[:, 0:1] * 256.0 + cols[:, 1:2]
        code = jnp.where(k_row < count, code, FAR)
        k_ref[part * rows : (part + 1) * rows, :] = jnp.broadcast_to(code, (rows, 128))


GRAD_STEPS = 8


def prepare_body(
    at_ref, modal_ref, doc_ref, weight_ref, grad_ref, q_ref, k_ref, out_ref, w_buf, g_buf, sems
):
    wide = w_buf.shape[1] // GRAD_STEPS
    copies = []
    for i in range(GRAD_STEPS):
        c = pl.ds(i * wide, wide)
        for n, (src, dst) in enumerate(
            ((weight_ref.at[at_ref[0], :, c], w_buf), (grad_ref.at[:, c], g_buf))
        ):
            copy = pltpu.make_async_copy(src, dst.at[:, c], sems.at[n, i])
            copy.start()
            copies.append(copy)
    codes_into(at_ref[0], modal_ref, doc_ref, q_ref, k_ref)
    total = jnp.zeros(out_ref.shape, F32)
    for i in range(GRAD_STEPS):
        copies[2 * i].wait()
        copies[2 * i + 1].wait()
        c = slice(i * wide, (i + 1) * wide)
        total = total + lax.dot_general(
            g_buf[:, c], w_buf[:, c], NT, preferred_element_type=F32
        )
    out_ref[...] = total.astype(BF)


def prepare(at, modality, doc_ids, out_weight, out_grad):
    _, cols, width = out_weight.shape
    rows = out_grad.shape[0]
    return pl.pallas_call(
        prepare_body,
        out_shape=(
            jax.ShapeDtypeStruct((8, rows), F32),
            jax.ShapeDtypeStruct((2 * rows, 128), F32),
            jax.ShapeDtypeStruct((rows, cols), BF),
        ),
        in_specs=[SMEM, VMEM, VMEM, HBM, HBM],
        out_specs=(VMEM,) * 3,
        scratch_shapes=[
            pltpu.VMEM((cols, width), BF),
            pltpu.VMEM((rows, width), BF),
            pltpu.SemaphoreType.DMA((2, GRAD_STEPS)),
        ],
        compiler_params=pltpu.CompilerParams(vmem_limit_bytes=50 * 1024 * 1024),
        cost_estimate=cost(2 * rows * cols * width, 2 * (cols + rows) * width),
        name="prepare",
    )(at, modality, doc_ids, out_weight, out_grad)


TILE = 256


def tile_scores(k_ref, peer_ref, q_ref, bias, c, r):
    keys = jnp.concatenate((k_ref[: r.stop, c], peer_ref[0, :, c]))
    s = lax.dot_general(keys, q_ref[r, c], NT, preferred_element_type=F32)
    return keys, s * (HD**-0.5 * LOG2E) + bias


def tile_bias(qc_ref, kc_ref, rows, r):
    code = jnp.concatenate((kc_ref[: r.stop], kc_ref[rows:]))
    code = jnp.concatenate([code] * (TILE // 128), axis=1)
    ok = (code >= qc_ref[0:1, r]) & (code <= qc_ref[1:2, r])
    return jnp.where(ok, 0.0, MASKED)


def forward_body(
    q_ref, k_ref, v_ref, peer_ref, qc_ref, kc_ref, spread_ref, total_ref, att_buf, sems
):
    rows, cols = q_ref.shape
    saves = []
    for t in range(0, rows, TILE):
        r = slice(t, t + TILE)
        bias = tile_bias(qc_ref, kc_ref, rows, r)
        for h in range(cols // HD):
            c = slice(h * HD, (h + 1) * HD)
            _, s = tile_scores(k_ref, peer_ref, q_ref, bias, c, r)
            values = jnp.concatenate((v_ref[: r.stop, c], peer_ref[1, :, c]))
            top = jnp.max(s, axis=0, keepdims=True)
            w = jnp.exp2(s - top)
            sums = jnp.sum(w, axis=0, keepdims=True)
            total_ref[h, :, r] = jnp.broadcast_to(top + jnp.log(sums) * LOG2E, (8, TILE))
            mixed = lax.dot_general(values, w.astype(BF), TN, preferred_element_type=F32)
            att_buf[r, c] = jnp.transpose(mixed / sums).astype(BF)
        for x in range(spread_ref.shape[0]):
            copy = pltpu.make_async_copy(att_buf.at[r], spread_ref.at[x, r], sems.at[len(saves)])
            copy.start()
            saves.append(copy)
    for copy in saves:
        copy.wait()


def forward(q, k, v, peer, codes, copies):
    rows, cols = q.shape
    heads = cols // HD
    return pl.pallas_call(
        forward_body,
        out_shape=(
            jax.ShapeDtypeStruct((copies, rows, cols), BF),
            jax.ShapeDtypeStruct((heads, 8, rows), F32),
        ),
        in_specs=[VMEM] * 6,
        out_specs=(HBM, VMEM),
        scratch_shapes=[
            pltpu.VMEM((rows, cols), BF),
            pltpu.SemaphoreType.DMA((copies * rows // TILE,)),
        ],
        compiler_params=pltpu.CompilerParams(vmem_limit_bytes=28 * 1024 * 1024),
        cost_estimate=cost(8 * heads * rows * rows * HD, 12 * rows * rows * heads),
        name="forward",
    )(q, k, v, peer, *codes)


def backward_body(
    q_ref,
    k_ref,
    v_ref,
    peer_ref,
    ga_ref,
    qc_ref,
    kc_ref,
    total_ref,
    spread_ref,
    dq_ref,
    own_ref,
    cross_ref,
    att_buf,
    sem,
):
    rows, cols = q_ref.shape
    factor = HD ** (-0.5)
    load = pltpu.make_async_copy(spread_ref.at[0], att_buf, sem)
    load.start()
    load.wait()
    biases = [tile_bias(qc_ref, kc_ref, rows, slice(t, t + TILE)) for t in range(0, rows, TILE)]
    for h in range(cols // HD):
        c = slice(h * HD, (h + 1) * HD)
        sums = []
        for n, t in enumerate(range(0, rows, TILE)):
            r = slice(t, t + TILE)
            keys, s = tile_scores(k_ref, peer_ref, q_ref, biases[n], c, r)
            values = jnp.concatenate((v_ref[: r.stop, c], peer_ref[1, :, c]))
            ga = ga_ref[r, c]
            both = ga.astype(F32) * att_buf[r, c].astype(F32)
            delta = jnp.sum(jnp.transpose(both), axis=0, keepdims=True)
            prob = jnp.exp2(s - total_ref[h, 0:1, r])
            dp = lax.dot_general(values, ga, NT, preferred_element_type=F32)
            ds = (prob * (dp - delta)).astype(BF)
            dq = lax.dot_general(keys, ds, TN, preferred_element_type=F32)
            dq_ref[r, c] = jnp.transpose(dq * factor).astype(BF)
            sums.append(
                (
                    jnp.dot(ds, q_ref[r, c], preferred_element_type=F32) * factor,
                    jnp.dot(prob.astype(BF), ga, preferred_element_type=F32),
                )
            )
        for n, (one, two) in enumerate(zip(*sums)):
            own = jnp.concatenate((one[:TILE] + two[:TILE], two[TILE:rows]))
            own_ref[n, :, c] = own.astype(BF)
            cross_ref[n, :, c] = (one[TILE:] + two[rows:]).astype(BF)


def backward(q, k, v, peer, ga, codes, total, spread):
    rows, cols = q.shape
    heads = cols // HD
    pair = jax.ShapeDtypeStruct((2, rows, cols), BF)
    return pl.pallas_call(
        backward_body,
        out_shape=(jax.ShapeDtypeStruct((rows, cols), BF), pair, pair),
        in_specs=[VMEM] * 8 + [HBM],
        out_specs=(VMEM,) * 3,
        scratch_shapes=[pltpu.VMEM((rows, cols), BF), pltpu.SemaphoreType.DMA],
        compiler_params=pltpu.CompilerParams(vmem_limit_bytes=60 * 1024 * 1024),
        cost_estimate=cost(20 * heads * rows * rows * HD, 12 * rows * rows * heads),
        name="backward",
    )(q, k, v, peer, ga, *codes, total, spread)


def project_body(at_ref, att_ref, mine_ref, other_ref, out_ref, buf_ref, sems):
    parts, rows, cols = att_ref.shape
    half = cols // 2
    lhs, saves = [], []
    for which in (at_ref[2], 1 - at_ref[2]):
        lanes = pl.ds(pl.multiple_of(which * half, half), half)
        lhs.append(jnp.concatenate([att_ref[x, :, lanes] for x in range(parts)], axis=1))
    for n in range(out_ref.shape[0]):
        c = slice(n * cols, (n + 1) * cols)
        total = jnp.zeros((rows, cols), F32)
        for left, right in zip(lhs, (mine_ref, other_ref)):
            right = jnp.concatenate([right[x, :, c] for x in range(parts)], axis=0)
            total = total + jnp.dot(left, right, preferred_element_type=F32)
        buf_ref[n] = total.astype(BF)
        saves.append(pltpu.make_async_copy(buf_ref.at[n], out_ref.at[n], sems.at[n]))
        saves[-1].start()
    for save in saves:
        save.wait()


def project(at, att, mine, other):
    parts, rows, cols = att.shape
    outs = mine.shape[2] // cols
    return pl.pallas_call(
        project_body,
        out_shape=jax.ShapeDtypeStruct((outs, rows, cols), BF),
        in_specs=[SMEM] + [VMEM] * 3,
        out_specs=HBM,
        scratch_shapes=[pltpu.VMEM((outs, rows, cols), BF), pltpu.SemaphoreType.DMA((outs,))],
        compiler_params=pltpu.CompilerParams(vmem_limit_bytes=12 * 1024 * 1024),
        cost_estimate=cost(2 * parts * rows * cols * outs * cols, 4 * mine.size + 4 * att.size),
        name="project",
    )(at, att, mine, other)


def finish_body(own_ref, back_ref, dk_ref, dv_ref):
    dk_ref[...] = (own_ref[0].astype(F32) + back_ref[0].astype(F32)).astype(BF)
    dv_ref[...] = (own_ref[1].astype(F32) + back_ref[1].astype(F32)).astype(BF)


def finish(own, back):
    shape = jax.ShapeDtypeStruct(own.shape[1:], BF)
    return pl.pallas_call(
        finish_body,
        out_shape=(shape, shape),
        in_specs=[VMEM] * 2,
        out_specs=(VMEM,) * 2,
        compiler_params=pltpu.CompilerParams(vmem_limit_bytes=60 * 1024 * 1024),
        cost_estimate=cost(own.size, 8 * own.size),
        name="finish",
    )(own, back)


def step(query_heads, key_heads, value_heads, modality, doc_ids, out_weight, out_grad):
    _, cols = query_heads.shape
    at = jnp.stack([lax.axis_index(a).astype(jnp.int32) for a in ("side", "x", "core")])
    swap = [(0, 1), (1, 0)]
    xs = lax.axis_size("x")
    peer = lax.ppermute(jnp.stack((key_heads, value_heads)), "side", swap)
    half, wide = cols // 2, out_weight.shape[2] // xs
    side, core = lax.axis_index("side"), lax.axis_index("core")
    slabs = jnp.concatenate(
        [
            lax.dynamic_slice(out_weight, (side, core * half, i * wide), (1, half, wide))
            for i in range(xs)
        ]
    )
    mine = lax.all_to_all(slabs, "x", 0, 0, tiled=True)
    modality, _ = lax.optimization_barrier((modality, slabs))
    query_code, key_code, grad_attended = prepare(
        at, modality, doc_ids, out_weight, out_grad
    )
    codes = (query_code, key_code)
    spread, total = forward(query_heads, key_heads, value_heads, peer, codes, xs)
    gathered = lax.all_to_all(spread, "x", 0, 0, tiled=True)
    other = lax.ppermute(mine, "core", swap)
    grad_query, own, cross = backward(
        query_heads, key_heads, value_heads, peer, grad_attended, codes, total, spread
    )
    returned = lax.ppermute(cross, "side", swap)
    partial = project(at, gathered, mine, other)
    pieces = lax.all_to_all(partial, "y", 0, 0, tiled=True)
    layer_output = jnp.sum(pieces.astype(F32), axis=0).astype(BF)
    grad_key, grad_value = finish(own, returned)
    return (layer_output, grad_query, grad_key, grad_value)


def solution(mesh):
    groups, _ = mesh.devices.shape
    split = Mesh(mesh.devices.reshape(2, groups // 4, 2, 4, 4), ("side", "z", "core", "x", "y"))
    grp, tp = ("side", "z", "core"), ("x", "y")
    tokens = P(grp, tp)
    placed = (
        tokens,
        tokens,
        tokens,
        P(grp, None),
        P(grp, None),
        P(None, tp, None),
        P(grp, None),
    )
    return jax.shard_map(
        step,
        mesh=split,
        in_specs=placed,
        out_specs=(tokens, tokens, tokens, tokens),
        check_vma=False,
    )
```
